32 devices in a mesh: group: 2 (over y), tile: 4 (over z), dp: 2 (over x), chan: 2 (over core).
Axes of the slice: x: 2, y: 2, z: 4, core: 2. Of those that a mesh axis runs over, the one named last changes fastest.
Arguments:
- inputs: bfloat16 [4, 4, 32, 32, 128], P(('group', 'dp'), 'tile'), parts along dimension 0, may hold values from -6 to 6
- kernel: float32 [49, 128], replicated, may hold values from -0.875 to 0.875
- norm_gain: float32 [128], replicated, may hold values from 0.1 to 1.9
- w_in: bfloat16 [128, 512], P(None, 'chan'), may hold values from -0.5 to 0.5
- w_out: bfloat16 [512, 128], P('chan'), may hold values from -0.25 to 0.25
- layer_scale: float32 [128], replicated, may hold values from 0.25 to 2
- cotangent: bfloat16 [4, 4, 32, 32, 128], P(('group', 'dp'), 'tile'), parts along dimension 0, may hold values from -6 to 6
- adjacency: int32 [4, 8, 2], replicated, may hold values from 0 to 3, as said below
Outputs:
- inputs_grad: bfloat16 [4, 4, 32, 32, 128], P(('group', 'dp'), 'tile'), parts along dimension 0
- kernel_grad: float32 [98, 128], P('group'), parts along dimension 0
- gain_grad: float32 [256], P('group'), parts along dimension 0
- w_in_grad: float32 [256, 512], P(('group', 'dp'), 'chan'), parts along dimension 0
- w_out_grad: float32 [1024, 128], P(('group', 'chan'), 'dp'), parts along dimension 0
- scale_grad: float32 [256], P('group'), parts along dimension 0
The draws below stay inside these ranges and needn't reach their ends.
There are 2 independent parts, one for each index of `group`. The reference program is written for one: setup_inputs(seed, part) draws one part's arguments, and reference() takes and returns one part's arrays. A program takes and returns all parts, laid end to end along the dimension named above; an argument that names none is the same for every part. Nothing has to cross between parts.
Inputs may be any that keep to these rules, and one draw needn't show every extreme that they name: adjacency[t, k, 0] is the tile beside tile t in direction k of t's own frame and adjacency[t, k, 1] the quarter turns relating the two frames, as in the reference program. The tiles form a closed band of two rows of 2 tiles, a stand-in for a sphere's tiling with rotated neighbours, with consistent neighbours; every tile is some tile's neighbour.
All inputs are finite; a program needn't handle non-finite values.
Results may differ from the reference program's by a relative error of at most 0.0063.
Values may be sent and summed in bfloat16 or wider, within the bound.
A program may use at most 64 MiB of HBM per device.

```python
import math
import jax
import jax.numpy as jnp
from jax import lax

C = 128
HID = 512
KS = 7
TS = 32
TILES = 4
BATCH = 2


def draw_adjacency(key, part):
    columns = TILES // 2
    placing = jax.random.permutation(jax.random.fold_in(key, 11), TILES).astype(jnp.int32)
    quarter_turns = jax.random.randint(jax.random.fold_in(key, 23), (TILES,), 0, 4, dtype=jnp.int32)
    tile_ids = jnp.arange(TILES, dtype=jnp.int32)
    at_cell = jnp.zeros((TILES,), jnp.int32).at[placing].set(tile_ids)
    grid_row = placing // columns
    grid_col = placing % columns
    step_rows = jnp.array([-1, 0, 1, 0, -1, 1, 1, -1], jnp.int32)
    step_cols = jnp.array([0, 1, 0, -1, 1, 1, -1, -1], jnp.int32)
    slot_ids = jnp.arange(8, dtype=jnp.int32)
    edge_dirs = (slot_ids[None, :] + quarter_turns[:, None]) % 4
    corner_dirs = 4 + (slot_ids[None, :] - 4 + quarter_turns[:, None]) % 4
    direction = jnp.where(slot_ids[None, :] < 4, edge_dirs, corner_dirs)
    neighbour_row = (grid_row[:, None] + step_rows[direction]) % 2
    neighbour_col = (grid_col[:, None] + step_cols[direction]) % columns
    neighbour = at_cell[neighbour_row * columns + neighbour_col]
    relative = (quarter_turns[:, None] - quarter_turns[neighbour]) % 4
    return jnp.stack([neighbour, relative], axis=-1).astype(jnp.int32)


def strengthened(drawn, key, source, target, blocks, factor):
    owner, partner = [(jnp.arange(drawn.shape[dim]) // (drawn.shape[dim] // blocks)).reshape([-1 if axis == dim else 1 for axis in range(drawn.ndim)]) for dim in (source, target)]
    chosen = jax.random.permutation(key, blocks)[partner]
    strong = (owner == chosen) | (owner == (partner + blocks // 2) % blocks)
    return jnp.where(strong, factor * drawn, drawn)


def block_levels(key, extent, shards, smallest, largest):
    gain = 1.0
    for dim, shards_of in shards:
        heights = jax.random.uniform(jax.random.fold_in(jax.random.fold_in(key, 6), dim), (shards_of,), jnp.float32, smallest / len(shards), largest / len(shards))
        gain = gain * jnp.repeat(jnp.exp(heights), extent[dim] // shards_of).reshape((-1,) + (1,) * (len(extent) - 1 - dim))
    return gain


def scatter_about(stream_key, shape, scale, bound, cuts=(), kind=jnp.bfloat16):
    result = jax.random.normal(stream_key, shape, jnp.float32) * scale
    if len(cuts) > 0:
        result = block_levels(stream_key, shape, cuts, -0.22, 0.18) * result
    return jnp.clip(result, min=-bound, max=bound).astype(kind)


def bell_draw_with(rng, shape, spread, reach, cuts, heavy, kind=jnp.bfloat16):
    entries = spread * jax.random.normal(rng, shape, jnp.float32)
    if cuts:
        entries = entries * block_levels(rng, shape, cuts, -0.22, 0.18)
    return jnp.clip(strengthened(entries, jax.random.fold_in(rng, 3), *heavy), -reach, reach).astype(kind)


def setup_inputs(seed: int = 0, part: int = 0) -> dict:
    key_list = jax.random.split(jax.random.key(seed), 9)
    own_keys = jax.random.split(jax.random.fold_in(key_list[8], part), 9)
    return {
        "inputs": scatter_about(own_keys[0], (BATCH, TILES, TS, TS, C), 1.0, 6.0, ((0, 2), (1, 4))),
        "kernel": scatter_about(key_list[1], (KS * KS, C), (KS * KS) ** -0.5, 0.875, (), jnp.float32),
        "norm_gain": jnp.clip(1.0 + 0.18 * jax.random.normal(key_list[2], (C,), jnp.float32), 0.1, 1.9),
        "w_in": scatter_about(key_list[3], (C, HID), C ** -0.5, 0.5, ((1, 2),)),
        "w_out": scatter_about(key_list[4], (HID, C), HID ** -0.5, 0.25, ((0, 2),)),
        "layer_scale": jnp.clip(jnp.exp(jax.random.uniform(key_list[5], (C,), jnp.float32, math.log(0.25), math.log(2.0))), 0.25, 2.0),
        "cotangent": bell_draw_with(own_keys[6], (BATCH, TILES, TS, TS, C), 1.0, 6.0, ((0, 2), (1, 4)), (0, 4, 2, 2.0)),
        "adjacency": draw_adjacency(jax.random.fold_in(key_list[8], 71), part),
    }


eps = 1e-06
root_two_pi = 0.7978845608028654
cubic_coef = 0.044715

def gelu_pair(values):
    inner = root_two_pi * (values + cubic_coef * values * values * values)
    tanh_part = jnp.tanh(inner)
    active = 0.5 * values * (1.0 + tanh_part)
    gelu_slope = 0.5 * (1.0 + tanh_part) + 0.5 * values * (1.0 - tanh_part * tanh_part) * root_two_pi * (1.0 + 3.0 * cubic_coef * values * values)
    return (active, gelu_slope)

def norm_forward(conv_flat, norm_gain):
    row_mean = lax.optimization_barrier(jnp.mean(conv_flat, axis=1, keepdims=True))
    centred = conv_flat - row_mean
    inv_std = lax.rsqrt(lax.optimization_barrier(jnp.mean(centred * centred, axis=1, keepdims=True)) + eps)
    normed = centred * inv_std
    return (normed, inv_std, (normed * norm_gain).astype(jnp.bfloat16))

def norm_backward(normed_grad, normed, inv_std, norm_gain):
    scaled = normed_grad * norm_gain
    first_mean = lax.optimization_barrier(jnp.mean(scaled, axis=1, keepdims=True))
    second_mean = lax.optimization_barrier(jnp.mean(scaled * normed, axis=1, keepdims=True))
    return (inv_std * (scaled - first_mean - normed * second_mean)).astype(jnp.bfloat16)

def pointwise(conv_flat, upstream_flat, norm_gain, w_in, w_out, layer_scale):
    normed, inv_std, normed_b = norm_forward(conv_flat, norm_gain)
    hidden = jnp.dot(normed_b, w_in, preferred_element_type=jnp.float32)
    active, gelu_slope = gelu_pair(hidden)
    active_b = active.astype(jnp.bfloat16)
    branch = jnp.dot(active_b, w_out, preferred_element_type=jnp.float32)
    scale_part = lax.optimization_barrier(jnp.sum(upstream_flat * branch, axis=0))
    scaled_b = (upstream_flat * layer_scale).astype(jnp.bfloat16)
    w_out_part = jnp.dot(active_b.T, scaled_b, preferred_element_type=jnp.float32)
    hidden_grad = (jnp.dot(scaled_b, w_out.T, preferred_element_type=jnp.float32) * gelu_slope).astype(jnp.bfloat16)
    w_in_part = jnp.dot(normed_b.T, hidden_grad, preferred_element_type=jnp.float32)
    normed_grad = jnp.dot(hidden_grad, w_in.T, preferred_element_type=jnp.float32)
    gain_part = lax.optimization_barrier(jnp.sum(normed_grad * normed, axis=0))
    conv_grad = norm_backward(normed_grad, normed, inv_std, norm_gain)
    return (conv_grad, w_in_part, w_out_part, gain_part, scale_part)

def depthwise(padded, kernel, first_row, row_count):
    rim_width = KS // 2
    rows = lax.dynamic_slice_in_dim(padded, first_row, row_count + 2 * rim_width, 1)
    tile_side = padded.shape[2] - 2 * rim_width
    summed = jnp.zeros((rows.shape[0], row_count, tile_side, rows.shape[3]), jnp.float32)
    for shift_row in range(KS):
        for shift_col in range(KS):
            summed = summed + rows[:, shift_row:shift_row + row_count, shift_col:shift_col + tile_side].astype(jnp.float32) * kernel[shift_row * KS + shift_col]
    return summed

def kernel_terms(rows, conv_grad):
    row_count, tile_side = (conv_grad.shape[1], conv_grad.shape[2])
    grad_f = conv_grad.astype(jnp.float32)
    terms = []
    for shift_row in range(KS):
        for shift_col in range(KS):
            window = rows[:, shift_row:shift_row + row_count, shift_col:shift_col + tile_side].astype(jnp.float32)
            terms.append(lax.optimization_barrier(jnp.sum(window * grad_f, axis=(0, 1, 2))))
    return jnp.stack(terms, axis=0)

def turned(image, quarter):
    options = [lambda values, count=count: jnp.rot90(values, count, axes=(1, 2)) for count in range(4)]
    return lax.switch(quarter, options, image)

def rim_regions(rim_width):
    near = slice(0, rim_width)
    far = slice(-rim_width, None)
    inner = slice(rim_width, -rim_width)
    whole = slice(None)
    return ((near, inner, far, whole), (inner, far, whole, near), (far, inner, near, whole), (inner, near, whole, far), (near, far, far, near), (far, far, near, near), (far, near, near, far), (near, near, far, far))

def padded_tile(inputs, adjacency, tile_id):
    rim_width = KS // 2
    pieces = []
    for slot_index in range(8):
        source = adjacency[tile_id, slot_index, 0]
        image = lax.dynamic_index_in_dim(inputs, source, 1, keepdims=False)
        pieces.append(turned(image, adjacency[tile_id, slot_index, 1]))
    north, east, south, west, north_east, south_east, south_west, north_west = pieces
    centre = lax.dynamic_index_in_dim(inputs, tile_id, 1, keepdims=False)
    top_rows = jnp.concatenate([north_west[:, -rim_width:, -rim_width:], north[:, -rim_width:, :], north_east[:, -rim_width:, :rim_width]], axis=2)
    middle_rows = jnp.concatenate([west[:, :, -rim_width:], centre, east[:, :, :rim_width]], axis=2)
    bottom_rows = jnp.concatenate([south_west[:, :rim_width, -rim_width:], south[:, :rim_width, :], south_east[:, :rim_width, :rim_width]], axis=2)
    return jnp.concatenate([top_rows, middle_rows, bottom_rows], axis=1)

def reference(inputs, kernel, norm_gain, w_in, w_out, layer_scale, cotangent, adjacency):
    rim_width = KS // 2
    channels = inputs.shape[4]

    def one_tile(tile_id):
        padded = padded_tile(inputs, adjacency, tile_id)
        upstream = lax.dynamic_index_in_dim(cotangent, tile_id, 1, keepdims=False)
        samples = upstream.shape[0]
        conv = depthwise(padded, kernel, 0, TS)
        conv_grad, w_in_part, w_out_part, gain_part, scale_part = pointwise(conv.reshape(-1, channels), upstream.reshape(-1, channels).astype(jnp.float32), norm_gain, w_in, w_out, layer_scale)
        conv_grad = conv_grad.reshape(samples, TS, TS, channels)
        kernel_part = kernel_terms(padded, conv_grad)
        pad_grad = jnp.zeros(padded.shape, jnp.float32)
        grad_f = conv_grad.astype(jnp.float32)
        for shift_row in range(KS):
            for shift_col in range(KS):
                pad_grad = pad_grad.at[:, shift_row:shift_row + TS, shift_col:shift_col + TS].add(kernel[shift_row * KS + shift_col] * grad_f)
        return (pad_grad, kernel_part, gain_part, w_in_part, w_out_part, scale_part)
    pad_grads, kernel_parts, gain_parts, w_in_parts, w_out_parts, scale_parts = lax.map(one_tile, jnp.arange(TILES, dtype=jnp.int32))
    regions = rim_regions(rim_width)
    summed = cotangent.astype(jnp.float32) + jnp.moveaxis(pad_grads[:, :, rim_width:-rim_width, rim_width:-rim_width], 0, 1)

    def route(tile_id, summed):
        slot_grads = lax.dynamic_index_in_dim(pad_grads, tile_id, 0, keepdims=False)
        for slot_index in range(8):
            pad_rows, pad_cols, image_rows, image_cols = regions[slot_index]
            placed = jnp.zeros((BATCH, TS, TS, channels), jnp.float32).at[:, image_rows, image_cols].set(slot_grads[:, pad_rows, pad_cols])
            back = turned(placed, (4 - adjacency[tile_id, slot_index, 1]) % 4)
            target = adjacency[tile_id, slot_index, 0]
            current = lax.dynamic_index_in_dim(summed, target, 1, keepdims=False)
            summed = lax.dynamic_update_index_in_dim(summed, current + back, target, 1)
        return summed
    summed = lax.fori_loop(0, TILES, route, summed)
    factor = 1.0 / math.sqrt(BATCH * TILES * TS * TS)
    return (summed.astype(jnp.bfloat16), lax.optimization_barrier(jnp.sum(kernel_parts, axis=0)) * factor, lax.optimization_barrier(jnp.sum(gain_parts, axis=0)) * factor, lax.optimization_barrier(jnp.sum(w_in_parts, axis=0)) * factor, lax.optimization_barrier(jnp.sum(w_out_parts, axis=0)) * factor, lax.optimization_barrier(jnp.sum(scale_parts, axis=0)) * factor)
```

```python
import functools
import math

import jax
import jax.numpy as jnp
from jax import lax
from jax.experimental import pallas as pl
from jax.experimental.pallas import tpu as pltpu
from jax.sharding import PartitionSpec as P

KS = 7
H = KS // 2
COL = 8
ROWS_AT_ONCE = 4
SMALL_ROWS = 56

eps = 1e-06
root_two_pi = 0.7978845608028654
cubic_coef = 0.044715
facing_turns = (2, 3, 0, 1, 2, 0, 0, 2)
corner_at_end = (True, False, True, False)
MESH = pl.DeviceIdType.MESH
F32 = jnp.float32
BF16 = jnp.bfloat16


def gelu_pair(values):
    square = values * values
    tanh_part = jnp.tanh(values * (root_two_pi + (root_two_pi * cubic_coef) * square))
    half_up = 0.5 + 0.5 * tanh_part
    active = values * half_up
    gelu_slope = half_up + active * (1.0 - tanh_part) * (
        root_two_pi + (3.0 * root_two_pi * cubic_coef) * square
    )
    return active, gelu_slope


def mm(left, right, left_dim, right_dim):
    return lax.dot_general(
        left, right, (((left_dim,), (right_dim,)), ((), ())), preferred_element_type=F32
    )


def body(
    tiles, dps, factor,
    adj, x_ref, ct_ref, kern, gain_ref, w_in_ref, w_out_ref, scale_ref,
    out_ref, small_out, w_out_all,
    pad, strips, faces, win, wout, conv_ref, part, cg, cpad, gpad, rimf, rims, incoming,
    chan_recv, dp_send, dp_recv, tile_grads, kacc, small_chan, small_dp, small_tile, base,
    face_send, face_recv, pair_send, pair_recv, rim_send, rim_recv,
    dp_send_sem, dp_recv_sem, tg_send, tg_recv, sd_send, sd_recv, st_send, st_recv,
):
    ts = x_ref.shape[0]
    half = ts // 2
    strip = H * ts
    me_t = lax.axis_index("tile")
    me_d = lax.axis_index("dp")
    me_c = lax.axis_index("chan")
    sib = 1 - me_c

    barrier = pltpu.get_barrier_semaphore()
    for o in range(1, tiles):
        pl.semaphore_signal(barrier, inc=1, device_id={"tile": lax.rem(me_t + o, tiles)}, device_id_type=MESH)
    for o in range(1, dps):
        pl.semaphore_signal(barrier, inc=1, device_id={"dp": lax.rem(me_d + o, dps)}, device_id_type=MESH)
    pl.semaphore_signal(barrier, inc=1, device_id={"chan": sib}, device_id_type=MESH)

    def to_peers(axis, size, me, source, target, send_sems, recv_sems):
        copies = []
        for o in range(1, size):
            peer = lax.rem(me + o, size)
            copy = pltpu.make_async_remote_copy(
                src_ref=source(peer), dst_ref=target, send_sem=send_sems.at[o - 1],
                recv_sem=recv_sems.at[o - 1], device_id={axis: peer}, device_id_type=MESH,
            )
            copy.start()
            copies.append(copy)
        return copies

    def to_sibling(source, target, index):
        copy = pltpu.make_async_remote_copy(
            src_ref=source, dst_ref=target, send_sem=pair_send.at[index],
            recv_sem=pair_recv.at[index], device_id={"chan": sib}, device_id_type=MESH,
        )
        copy.start()
        return copy

    def rows_loop(count, step):
        def wrapped(index, carry):
            step(index)
            return carry
        lax.fori_loop(0, count, wrapped, 0)

    def fill(i):
        pad[H + i, COL:COL + ts, :] = x_ref[i].astype(F32)
    rows_loop(ts, fill)
    for d in range(H):
        strips[0, d * ts:(d + 1) * ts, :] = x_ref[d].astype(F32)

    def face_row(p):
        for d in range(H):
            strips[1, pl.ds(d * ts + p, 1), :] = pad[H + p, COL + ts - 1 - d:COL + ts - d, :]
            strips[2, pl.ds(d * ts + p, 1), :] = pad[H + ts - 1 - d, pl.ds(COL + ts - 1 - p, 1), :]
            strips[3, pl.ds(d * ts + p, 1), :] = pad[H + ts - 1 - p, COL + d:COL + d + 1, :]
    rows_loop(ts, face_row)
    for f in range(4):
        faces[me_t, f] = strips[f].astype(BF16)
    win[me_c] = w_in_ref[...]
    wout[me_c] = w_out_ref[...]

    pl.semaphore_wait(barrier, tiles - 1 + dps - 1 + 1)
    face_copies = to_peers("tile", tiles, me_t, lambda peer: faces.at[me_t], faces.at[me_t], face_send, face_recv)
    win_copy = to_sibling(win.at[me_c], win.at[me_c], 0)
    wout_copy = to_sibling(wout.at[me_c], wout.at[me_c], 1)

    def zero_rows(i):
        cpad[i] = jnp.zeros(cpad.shape[1:], F32)
    rows_loop(cpad.shape[0], zero_rows)
    kacc[...] = jnp.zeros_like(kacc)

    for copy in face_copies:
        copy.wait_recv()

    for k in range(8):
        source = adj[me_t, k, 0]
        face = (adj[me_t, k, 1] + facing_turns[k]) % 4
        strips[k] = faces[source, face].astype(F32)
    for d in range(H):
        pad[H + ts + d, COL:COL + ts, :] = strips[2, d * ts:(d + 1) * ts, :]

    def rim_row(p):
        for d in range(H):
            pad[d, pl.ds(COL + p, 1), :] = strips[0, pl.ds((H - 1 - d) * ts + ts - 1 - p, 1), :]
            pad[H + p, COL + ts + d:COL + ts + d + 1, :] = strips[1, pl.ds(d * ts + ts - 1 - p, 1), :]
            pad[H + p, COL - H + d:COL - H + d + 1, :] = strips[3, pl.ds((H - 1 - d) * ts + p, 1), :]
    rows_loop(ts, rim_row)
    for i in range(H):
        for j in range(H):
            at = (H - 1 - i) * ts + ts - H + (H - 1 - j)
            pad[i, COL + ts + j:COL + ts + j + 1, :] = strips[4, at:at + 1, :]
            at = i * ts + j
            pad[H + ts + i, COL + ts + j:COL + ts + j + 1, :] = strips[5, at:at + 1, :]
            at = i * ts + ts - H + j
            pad[H + ts + i, COL - H + j:COL - H + j + 1, :] = strips[6, at:at + 1, :]
            at = (H - 1 - i) * ts + (H - 1 - j)
            pad[i, COL - H + j:COL - H + j + 1, :] = strips[7, at:at + 1, :]

    first = me_c * half

    def conv_rows(block):
        i = block * ROWS_AT_ONCE
        acc = [jnp.zeros((ts, pad.shape[2]), F32) for _ in range(ROWS_AT_ONCE)]
        for a in range(ROWS_AT_ONCE + KS - 1):
            for b in range(KS):
                window = pad[first + i + a, COL - H + b:COL - H + b + ts, :]
                for r in range(ROWS_AT_ONCE):
                    if 0 <= a - r < KS:
                        at = (a - r) * KS + b
                        acc[r] = acc[r] + window * kern[at:at + 1, :]
        for r in range(ROWS_AT_ONCE):
            conv_ref[i + r] = acc[r]
    rows_loop(half // ROWS_AT_ONCE, conv_rows)

    win_copy.wait_recv()
    wout_copy.wait_recv()

    gain = gain_ref[...]
    layer_scale = scale_ref[...]
    block_rows = 8
    pixels = block_rows * ts
    channels = pad.shape[2]
    gain_total = jnp.zeros((1, channels), F32)
    scale_total = jnp.zeros((1, channels), F32)
    for block in range(half // block_rows):
        at = block * block_rows
        conv = conv_ref[at:at + block_rows].reshape(pixels, channels)
        mean = jnp.mean(conv, axis=1, keepdims=True)
        centred = conv - mean
        inv_std = lax.rsqrt(jnp.mean(centred * centred, axis=1, keepdims=True) + eps)
        normed = centred * inv_std
        normed_b = (normed * gain).astype(BF16)
        upstream = ct_ref[pl.ds(first + at, block_rows)].reshape(pixels, channels).astype(F32)
        scaled_b = (upstream * layer_scale).astype(BF16)
        branch = jnp.zeros((pixels, channels), F32)
        normed_grad = jnp.zeros((pixels, channels), F32)
        for c in range(2):
            active, slope = gelu_pair(mm(normed_b, win[c], 1, 0))
            active_b = active.astype(BF16)
            branch = branch + mm(active_b, wout[c], 1, 0)
            hidden_grad = (mm(scaled_b, wout[c], 1, 1) * slope).astype(BF16)
            normed_grad = normed_grad + mm(hidden_grad, win[c], 1, 1)
            in_grad = mm(normed_b, hidden_grad, 0, 0)
            out_grad = mm(scaled_b, active_b, 0, 0)
            if block == 0:
                part[c, 0] = in_grad
                part[c, 1] = out_grad
            else:
                part[c, 0] += in_grad
                part[c, 1] += out_grad
        scale_total = scale_total + jnp.sum(upstream * branch, axis=0, keepdims=True)
        gain_total = gain_total + jnp.sum(normed_grad * normed, axis=0, keepdims=True)
        scaled = normed_grad * gain
        first_mean = jnp.mean(scaled, axis=1, keepdims=True)
        second_mean = jnp.mean(scaled * normed, axis=1, keepdims=True)
        grad_b = (inv_std * (scaled - first_mean - normed * second_mean)).astype(BF16)
        cg[pl.ds(first + at, block_rows)] = grad_b.reshape(block_rows, ts, channels)

    cg_copy = to_sibling(cg.at[pl.ds(first, half)], cg.at[pl.ds(first, half)], 2)
    part_copy = to_sibling(part.at[sib], chan_recv, 3)

    for a in range(KS):
        def kernel_row(i, acc):
            grad = cg[first + i].astype(F32)
            new = []
            for b in range(KS):
                window = pad[first + i + a, COL - H + b:COL - H + b + ts, :]
                new.append(acc[b] + jnp.sum((window * grad).reshape(ts // 8, 8, channels), axis=0))
            return tuple(new)
        sums = lax.fori_loop(0, half, kernel_row, tuple(jnp.zeros((8, channels), F32) for _ in range(KS)))
        for b in range(KS):
            kacc[a * KS + b] = sums[b]
    small_chan[0] = jnp.sum(kacc[...], axis=1)
    small_chan[0, KS * KS:KS * KS + 1, :] = gain_total
    small_chan[0, KS * KS + 1:KS * KS + 2, :] = scale_total
    small_copy = to_sibling(small_chan.at[0], small_chan.at[1], 4)

    cg_copy.wait_recv()

    def widen(i):
        cpad[KS - 1 + i, COL:COL + ts, :] = cg[i].astype(F32)
    rows_loop(ts, widen)
    wide = gpad.shape[1]

    def spread_rows(block):
        i = block * 2
        acc = [jnp.zeros((wide, channels), F32) for _ in range(2)]
        for a in range(KS + 1):
            for b in range(KS):
                window = cpad[i + a, COL - (KS - 1) + b:COL - (KS - 1) + b + wide, :]
                for r in range(2):
                    if 0 <= a - r < KS:
                        at = (KS - 1 - (a - r)) * KS + KS - 1 - b
                        acc[r] = acc[r] + window * kern[at:at + 1, :]
        for r in range(2):
            gpad[i + r] = acc[r]
    rows_loop((ts + 2 * H) // 2, spread_rows)

    def edge_row(p):
        for d in range(H):
            rimf[pl.ds(d * ts + p, 1), :] = gpad[H - 1 - d, pl.ds(H + ts - 1 - p, 1), :]
            rimf[pl.ds(strip + d * ts + p, 1), :] = gpad[H + ts - 1 - p, H + ts + d:H + ts + d + 1, :]
            rimf[pl.ds(3 * strip + d * ts + p, 1), :] = gpad[H + p, H - 1 - d:H - d, :]
    rows_loop(ts, edge_row)
    rimf[4 * strip:, :] = jnp.zeros((64, channels), F32)
    for d in range(H):
        rimf[2 * strip + d * ts:2 * strip + (d + 1) * ts, :] = gpad[H + ts + d, H:H + ts, :]
    for i in range(H):
        for j in range(H):
            spots = (
                (H - 1 - i, H + ts + H - 1 - j), (H + ts + i, H + ts + j),
                (H + ts + i, j), (H - 1 - i, H - 1 - j),
            )
            for k in range(4):
                at = 4 * strip + 16 * k + H * i + j
                row, col = spots[k]
                rimf[at:at + 1, :] = gpad[row, col:col + 1, :]
    rims[me_t] = rimf[...].astype(BF16)
    rim_copies = to_peers("tile", tiles, me_t, lambda peer: rims.at[me_t], rims.at[me_t], rim_send, rim_recv)

    part_rows = channels // dps
    part_copy.wait_recv()
    for w in range(2):
        for d in range(dps):
            rows = slice(d * part_rows, (d + 1) * part_rows)
            dp_send[d, w] = part[me_c, w, rows, :] + chan_recv[w, rows, :]
    dp_recv[me_d] = dp_send[me_d]
    dp_copies = to_peers("dp", dps, me_d, lambda peer: dp_send.at[peer], dp_recv.at[me_d], dp_send_sem, dp_recv_sem)
    small_copy.wait_recv()
    small_dp[me_d] = small_chan[0] + small_chan[1]
    sd_copies = to_peers("dp", dps, me_d, lambda peer: small_dp.at[me_d], small_dp.at[me_d], sd_send, sd_recv)

    def base_row(i):
        base[i] = ct_ref[i].astype(F32) + gpad[H + i, H:H + ts, :]
    rows_loop(ts, base_row)

    for copy in dp_copies:
        copy.wait_recv()
    total = dp_recv[0]
    for d in range(1, dps):
        total = total + dp_recv[d]
    tile_grads[me_t] = total.astype(tile_grads.dtype)
    tg_copies = to_peers("tile", tiles, me_t, lambda peer: tile_grads.at[me_t], tile_grads.at[me_t], tg_send, tg_recv)
    for copy in sd_copies:
        copy.wait_recv()
    total = small_dp[0]
    for d in range(1, dps):
        total = total + small_dp[d]
    small_tile[me_t] = total
    st_copies = to_peers("tile", tiles, me_t, lambda peer: small_tile.at[me_t], small_tile.at[me_t], st_send, st_recv)

    for copy in rim_copies:
        copy.wait_recv()
    for f in range(4):
        def gather(p, carry):
            edge, at_start, at_end = carry
            for k in range(8):
                face = (adj[p, k, 1] + facing_turns[k]) % 4
                chosen = jnp.where((adj[p, k, 0] == me_t) & (face == f), 1.0, 0.0).astype(F32)
                if k < 4:
                    edge = edge + chosen * rims[p, strip * k:strip * (k + 1), :].astype(F32)
                else:
                    at = 4 * strip + 16 * (k - 4)
                    piece = chosen * rims[p, at:at + 16, :].astype(F32)
                    if corner_at_end[k - 4]:
                        at_end = at_end + piece
                    else:
                        at_start = at_start + piece
            return edge, at_start, at_end
        zero = jnp.zeros((16, channels), F32)
        edge, at_start, at_end = lax.fori_loop(0, tiles, gather, (jnp.zeros((strip, channels), F32), zero, zero))
        incoming[f] = edge
        for d in range(H):
            incoming[f, d * ts:d * ts + H, :] += at_start[d * H:(d + 1) * H]
            incoming[f, (d + 1) * ts - H:(d + 1) * ts, :] += at_end[d * H:(d + 1) * H]
    for d in range(H):
        base[d] += incoming[0, d * ts:(d + 1) * ts, :]

    def add_row(p):
        for d in range(H):
            base[p, ts - H + d:ts - H + d + 1, :] += incoming[1, pl.ds((H - 1 - d) * ts + p, 1), :]
            base[ts - H + d, pl.ds(p, 1), :] += incoming[2, pl.ds((H - 1 - d) * ts + ts - 1 - p, 1), :]
            base[p, d:d + 1, :] += incoming[3, pl.ds(d * ts + ts - 1 - p, 1), :]
    rows_loop(ts, add_row)

    def out_row(i):
        out_ref[i] = base[i].astype(BF16)
    rows_loop(ts, out_row)

    for copy in tg_copies:
        copy.wait_recv()
    total = tile_grads[0].astype(F32)
    for t in range(1, tiles):
        total = total + tile_grads[t].astype(F32)
    w_out_all[...] = total * factor
    for copy in st_copies:
        copy.wait_recv()
    total = small_tile[0]
    for t in range(1, tiles):
        total = total + small_tile[t]
    small_out[...] = total * factor

    for copy in face_copies + rim_copies + dp_copies + sd_copies + tg_copies + st_copies + [
        win_copy, wout_copy, cg_copy, part_copy, small_copy
    ]:
        copy.wait_send()


def on_device(inputs, kernel, norm_gain, w_in, w_out, layer_scale, cotangent, adjacency):
    ts, ch = inputs.shape[2], inputs.shape[4]
    hid = w_in.shape[1]
    tiles, dps = lax.axis_size("tile"), lax.axis_size("dp")
    factor = 1.0 / math.sqrt(dps * tiles * ts * ts)
    strip = H * ts
    rim_rows = 4 * strip + 64
    part_rows = ch // dps
    vmem = pl.BlockSpec(memory_space=pltpu.VMEM)
    dma = pltpu.SemaphoreType.DMA
    peers_t, peers_d = max(tiles - 1, 1), max(dps - 1, 1)
    out, small, grads = pl.pallas_call(
        functools.partial(body, tiles, dps, factor),
        out_shape=(
            jax.ShapeDtypeStruct((ts, ts, ch), BF16),
            jax.ShapeDtypeStruct((SMALL_ROWS, ch), F32),
            jax.ShapeDtypeStruct((2, part_rows, hid), F32),
        ),
        in_specs=[pl.BlockSpec(memory_space=pltpu.SMEM)] + [vmem] * 7,
        out_specs=(vmem,) * 3,
        scratch_shapes=[
            pltpu.VMEM((ts + 2 * H, ts + 2 * COL, ch), F32),
            pltpu.VMEM((8, strip, ch), F32),
            pltpu.VMEM((tiles, 4, strip, ch), BF16),
            pltpu.VMEM((2, ch, hid), BF16),
            pltpu.VMEM((2, hid, ch), BF16),
            pltpu.VMEM((ts // 2, ts, ch), F32),
            pltpu.VMEM((2, 2, ch, hid), F32),
            pltpu.VMEM((ts, ts, ch), BF16),
            pltpu.VMEM((ts + 2 * (KS - 1), ts + 2 * COL, ch), F32),
            pltpu.VMEM((ts + 2 * H, ts + 8, ch), F32),
            pltpu.VMEM((rim_rows, ch), F32),
            pltpu.VMEM((tiles, rim_rows, ch), BF16),
            pltpu.VMEM((4, strip, ch), F32),
            pltpu.VMEM((2, ch, hid), F32),
            pltpu.VMEM((dps, 2, part_rows, hid), F32),
            pltpu.VMEM((dps, 2, part_rows, hid), F32),
            pltpu.VMEM((tiles, 2, part_rows, hid), BF16),
            pltpu.VMEM((SMALL_ROWS, 8, ch), F32),
            pltpu.VMEM((2, SMALL_ROWS, ch), F32),
            pltpu.VMEM((dps, SMALL_ROWS, ch), F32),
            pltpu.VMEM((tiles, SMALL_ROWS, ch), F32),
            pltpu.VMEM((ts, ts, ch), F32),
            dma((peers_t,)), dma((peers_t,)), dma((5,)), dma((5,)), dma((peers_t,)), dma((peers_t,)),
            dma((peers_d,)), dma((peers_d,)), dma((peers_t,)), dma((peers_t,)),
            dma((peers_d,)), dma((peers_d,)), dma((peers_t,)), dma((peers_t,)),
        ],
        compiler_params=pltpu.CompilerParams(
            collective_id=0, has_side_effects=True, vmem_limit_bytes=48 * 1024 * 1024
        ),
    )(
        adjacency, inputs[0, 0], cotangent[0, 0], kernel, norm_gain[None], w_in, w_out, layer_scale[None]
    )
    taps = KS * KS
    return (
        out[None, None],
        small[:taps],
        small[taps],
        grads[0],
        grads[1].T,
        small[taps + 1],
    )


def solution(mesh):
    placed = (
        P(("group", "dp"), "tile", None, None, None),
        P(),
        P(),
        P(None, "chan"),
        P("chan", None),
        P(),
        P(("group", "dp"), "tile", None, None, None),
        P(),
    )
    return jax.shard_map(
        on_device,
        mesh=mesh,
        in_specs=placed,
        out_specs=(
            P(("group", "dp"), "tile", None, None, None),
            P("group", None),
            P("group"),
            P(("group", "dp"), "chan"),
            P(("group", "chan"), "dp"),
            P("group"),
        ),
        check_vma=False,
    )
```

```python
import functools
import math

import jax
import jax.numpy as jnp
from jax import lax
from jax.experimental import pallas as pl
from jax.experimental.pallas import tpu as pltpu
from jax.sharding import PartitionSpec as P

KS = 7
H = KS // 2
COL = 8
ROWS_AT_ONCE = 4
SMALL_ROWS = 64

eps = 1e-06
root_two_pi = 0.7978845608028654
cubic_coef = 0.044715
facing_turns = (2, 3, 0, 1, 2, 0, 0, 2)
corner_at_end = (True, False, True, False)
MESH = pl.DeviceIdType.MESH
F32 = jnp.float32
BF16 = jnp.bfloat16


def gelu_pair(values):
    square = values * values
    tanh_part = jnp.tanh(values * (root_two_pi + (root_two_pi * cubic_coef) * square))
    half_up = 0.5 + 0.5 * tanh_part
    active = values * half_up
    gelu_slope = half_up + active * (1.0 - tanh_part) * (
        root_two_pi + (3.0 * root_two_pi * cubic_coef) * square
    )
    return active, gelu_slope


def mm(left, right, left_dim, right_dim):
    return lax.dot_general(
        left, right, (((left_dim,), (right_dim,)), ((), ())), preferred_element_type=F32
    )


def body(
    tiles, dps, factor,
    adj, x_hbm, ct_hbm, kern, gain_ref, w_in_ref, w_out_ref, scale_ref,
    out_ref, small_out, w_out_all,
    pad, strips, faces, win, wout, conv_ref, part, cg, cpad, gpad, rimf, rims, incoming,
    chan_recv, dp_send, dp_recv, piece_send, piece_recv, piece_all, kacc, small_part, small_recv,
    small_dp, small_tile, small_done, base, x_ref, ct_ref, local_sem,
    face_send, face_recv, pair_send, pair_recv, rim_send, rim_recv,
    dp_send_sem, dp_recv_sem, rs_send, rs_recv, tg_send, tg_recv, sd_send, sd_recv, st_send, st_recv,
):
    ts = x_ref.shape[0]
    half = ts // 2
    strip = H * ts
    me_t = lax.axis_index("tile")
    me_d = lax.axis_index("dp")
    me_c = lax.axis_index("chan")
    sib = 1 - me_c

    x_copy = pltpu.make_async_copy(x_hbm, x_ref, local_sem.at[0])
    x_copy.start()
    win_local = pltpu.make_async_copy(w_in_ref, win.at[me_c], local_sem.at[1])
    win_local.start()
    wout_local = pltpu.make_async_copy(w_out_ref, wout.at[me_c], local_sem.at[2])
    wout_local.start()
    ct_copy = pltpu.make_async_copy(ct_hbm, ct_ref, local_sem.at[3])
    ct_copy.start()

    barrier = pltpu.get_barrier_semaphore()
    for o in range(1, tiles):
        pl.semaphore_signal(barrier, inc=1, device_id={"tile": lax.rem(me_t + o, tiles)}, device_id_type=MESH)
    for o in range(1, dps):
        pl.semaphore_signal(barrier, inc=1, device_id={"dp": lax.rem(me_d + o, dps)}, device_id_type=MESH)
    pl.semaphore_signal(barrier, inc=1, device_id={"chan": sib}, device_id_type=MESH)

    def to_peers(axis, size, me, source, target, send_sems, recv_sems):
        copies = []
        for o in range(1, size):
            peer = lax.rem(me + o, size)
            copy = pltpu.make_async_remote_copy(
                src_ref=source(peer), dst_ref=target, send_sem=send_sems.at[o - 1],
                recv_sem=recv_sems.at[o - 1], device_id={axis: peer}, device_id_type=MESH,
            )
            copy.start()
            copies.append(copy)
        return copies

    def to_sibling(source, target, index):
        copy = pltpu.make_async_remote_copy(
            src_ref=source, dst_ref=target, send_sem=pair_send.at[index],
            recv_sem=pair_recv.at[index], device_id={"chan": sib}, device_id_type=MESH,
        )
        copy.start()
        return copy

    def rows_loop(count, step):
        def wrapped(index, carry):
            step(index)
            return carry
        lax.fori_loop(0, count, wrapped, 0)

    x_copy.wait()

    def fill(i):
        pad[H + i, COL:COL + ts, :] = x_ref[i].astype(F32)
    rows_loop(ts, fill)
    for d in range(H):
        strips[0, d * ts:(d + 1) * ts, :] = x_ref[d].astype(F32)

    def face_row(p):
        for d in range(H):
            strips[1, pl.ds(d * ts + p, 1), :] = pad[H + p, COL + ts - 1 - d:COL + ts - d, :]
            strips[2, pl.ds(d * ts + p, 1), :] = pad[H + ts - 1 - d, pl.ds(COL + ts - 1 - p, 1), :]
            strips[3, pl.ds(d * ts + p, 1), :] = pad[H + ts - 1 - p, COL + d:COL + d + 1, :]
    rows_loop(ts, face_row)
    for f in range(4):
        faces[me_t, f] = strips[f].astype(BF16)

    pl.semaphore_wait(barrier, tiles - 1 + dps - 1 + 1)
    mine = pl.ds(2 * me_c, 2)
    face_copies = to_peers("tile", tiles, me_t, lambda peer: faces.at[me_t, mine], faces.at[me_t, mine], face_send, face_recv)
    win_copy = to_sibling(w_in_ref, win.at[me_c], 0)
    wout_copy = to_sibling(w_out_ref, wout.at[me_c], 1)

    def zero_rows(i):
        cpad[i] = jnp.zeros(cpad.shape[1:], F32)
    rows_loop(cpad.shape[0], zero_rows)
    kacc[...] = jnp.zeros_like(kacc)

    face_passes = []
    for o in range(1, tiles):
        face_copies[o - 1].wait_recv()
        source = lax.rem(me_t - o + tiles, tiles)
        face_passes.append(to_sibling(faces.at[source, mine], faces.at[source, mine], 5 + o))
    for copy in face_passes:
        copy.wait_recv()

    for k in range(8):
        source = adj[me_t, k, 0]
        face = (adj[me_t, k, 1] + facing_turns[k]) % 4
        strips[k] = faces[source, face].astype(F32)
    for d in range(H):
        pad[H + ts + d, COL:COL + ts, :] = strips[2, d * ts:(d + 1) * ts, :]

    def rim_row(p):
        for d in range(H):
            pad[d, pl.ds(COL + p, 1), :] = strips[0, pl.ds((H - 1 - d) * ts + ts - 1 - p, 1), :]
            pad[H + p, COL + ts + d:COL + ts + d + 1, :] = strips[1, pl.ds(d * ts + ts - 1 - p, 1), :]
            pad[H + p, COL - H + d:COL - H + d + 1, :] = strips[3, pl.ds((H - 1 - d) * ts + p, 1), :]
    rows_loop(ts, rim_row)
    for i in range(H):
        for j in range(H):
            at = (H - 1 - i) * ts + ts - H + (H - 1 - j)
            pad[i, COL + ts + j:COL + ts + j + 1, :] = strips[4, at:at + 1, :]
            at = i * ts + j
            pad[H + ts + i, COL + ts + j:COL + ts + j + 1, :] = strips[5, at:at + 1, :]
            at = i * ts + ts - H + j
            pad[H + ts + i, COL - H + j:COL - H + j + 1, :] = strips[6, at:at + 1, :]
            at = (H - 1 - i) * ts + (H - 1 - j)
            pad[i, COL - H + j:COL - H + j + 1, :] = strips[7, at:at + 1, :]

    first = me_c * half

    def conv_rows(block):
        i = block * ROWS_AT_ONCE
        acc = [jnp.zeros((ts, pad.shape[2]), F32) for _ in range(ROWS_AT_ONCE)]
        for a in range(ROWS_AT_ONCE + KS - 1):
            for b in range(KS):
                window = pad[first + i + a, COL - H + b:COL - H + b + ts, :]
                for r in range(ROWS_AT_ONCE):
                    if 0 <= a - r < KS:
                        at = (a - r) * KS + b
                        acc[r] = acc[r] + window * kern[at:at + 1, :]
        for r in range(ROWS_AT_ONCE):
            conv_ref[i + r] = acc[r]
    rows_loop(half // ROWS_AT_ONCE, conv_rows)

    win_copy.wait_recv()
    wout_copy.wait_recv()
    win_local.wait()
    wout_local.wait()
    ct_copy.wait()

    gain = gain_ref[...]
    layer_scale = scale_ref[...]
    block_rows = 8
    pixels = block_rows * ts
    channels = pad.shape[2]
    gain_total = jnp.zeros((1, channels), F32)
    scale_total = jnp.zeros((1, channels), F32)
    for block in range(half // block_rows):
        at = block * block_rows
        conv = conv_ref[at:at + block_rows].reshape(pixels, channels)
        mean = jnp.mean(conv, axis=1, keepdims=True)
        centred = conv - mean
        inv_std = lax.rsqrt(jnp.mean(centred * centred, axis=1, keepdims=True) + eps)
        normed = centred * inv_std
        normed_b = (normed * gain).astype(BF16)
        upstream = ct_ref[pl.ds(first + at, block_rows)].reshape(pixels, channels).astype(F32)
        scaled_b = (upstream * layer_scale).astype(BF16)
        branch = jnp.zeros((pixels, channels), F32)
        normed_grad = jnp.zeros((pixels, channels), F32)
        for c in range(2):
            active, slope = gelu_pair(mm(normed_b, win[c], 1, 0))
            active_b = active.astype(BF16)
            branch = branch + mm(active_b, wout[c], 1, 0)
            hidden_grad = (mm(scaled_b, wout[c], 1, 1) * slope).astype(BF16)
            normed_grad = normed_grad + mm(hidden_grad, win[c], 1, 1)
            in_grad = mm(normed_b, hidden_grad, 0, 0)
            out_grad = mm(scaled_b, active_b, 0, 0)
            if block == 0:
                part[c, 0] = in_grad
                part[c, 1] = out_grad
            else:
                part[c, 0] += in_grad
                part[c, 1] += out_grad
        scale_total = scale_total + jnp.sum(upstream * branch, axis=0, keepdims=True)
        gain_total = gain_total + jnp.sum(normed_grad * normed, axis=0, keepdims=True)
        scaled = normed_grad * gain
        first_mean = jnp.mean(scaled, axis=1, keepdims=True)
        second_mean = jnp.mean(scaled * normed, axis=1, keepdims=True)
        grad_b = (inv_std * (scaled - first_mean - normed * second_mean)).astype(BF16)
        cg[pl.ds(first + at, block_rows)] = grad_b.reshape(block_rows, ts, channels)

    cg_copy = to_sibling(cg.at[pl.ds(first, half)], cg.at[pl.ds(first, half)], 2)
    part_copy = to_sibling(part.at[sib], chan_recv, 3)

    for a in range(KS):
        def kernel_row(i, acc):
            grad = cg[first + i].astype(F32)
            new = []
            for b in range(KS):
                window = pad[first + i + a, COL - H + b:COL - H + b + ts, :]
                new.append(acc[b] + jnp.sum((window * grad).reshape(ts // 8, 8, channels), axis=0))
            return tuple(new)
        sums = lax.fori_loop(0, half, kernel_row, tuple(jnp.zeros((8, channels), F32) for _ in range(KS)))
        for b in range(KS):
            kacc[a * KS + b] = sums[b]
    for c in range(2):
        small_part[c] = jnp.sum(kacc[c * SMALL_ROWS // 2:(c + 1) * SMALL_ROWS // 2], axis=1)
    at = KS * KS - SMALL_ROWS // 2
    small_part[1, at:at + 1, :] = gain_total
    small_part[1, at + 1:at + 2, :] = scale_total
    small_copy = to_sibling(small_part.at[sib], small_recv, 4)

    part_rows = channels // dps
    part_copy.wait_recv()
    for w in range(2):
        for d in range(dps):
            rows = slice(d * part_rows, (d + 1) * part_rows)
            dp_send[d, w] = part[me_c, w, rows, :] + chan_recv[w, rows, :]
    dp_recv[me_d] = dp_send[me_d]
    dp_copies = to_peers("dp", dps, me_d, lambda peer: dp_send.at[peer], dp_recv.at[me_d], dp_send_sem, dp_recv_sem)
    small_copy.wait_recv()
    small_dp[me_d] = small_part[me_c] + small_recv[...]
    sd_copies = to_peers("dp", dps, me_d, lambda peer: small_dp.at[me_d], small_dp.at[me_d], sd_send, sd_recv)

    cg_copy.wait_recv()

    def widen(i):
        cpad[KS - 1 + i, COL:COL + ts, :] = cg[i].astype(F32)
    rows_loop(ts, widen)
    wide = gpad.shape[1]

    def spread_rows(block):
        i = block * 2
        acc = [jnp.zeros((wide, channels), F32) for _ in range(2)]
        for a in range(KS + 1):
            for b in range(KS):
                window = cpad[i + a, COL - (KS - 1) + b:COL - (KS - 1) + b + wide, :]
                for r in range(2):
                    if 0 <= a - r < KS:
                        at = (KS - 1 - (a - r)) * KS + KS - 1 - b
                        acc[r] = acc[r] + window * kern[at:at + 1, :]
        for r in range(2):
            gpad[i + r] = acc[r]
    spread_blocks = (ts + 2 * H) // 2
    rows_loop(spread_blocks // 2, spread_rows)

    piece_rows = 2 * part_rows // tiles
    for copy in dp_copies:
        copy.wait_recv()
    total = dp_recv[0]
    for d in range(1, dps):
        total = total + dp_recv[d]
    total = total.reshape(2 * part_rows, total.shape[2]).astype(BF16)
    for t in range(tiles):
        piece_send[t] = total[t * piece_rows:(t + 1) * piece_rows]
    piece_recv[me_t] = piece_send[me_t]
    rs_copies = to_peers("tile", tiles, me_t, lambda peer: piece_send.at[peer], piece_recv.at[me_t], rs_send, rs_recv)
    for copy in sd_copies:
        copy.wait_recv()
    total = small_dp[0]
    for d in range(1, dps):
        total = total + small_dp[d]
    small_tile[me_t] = total
    st_copies = to_peers("tile", tiles, me_t, lambda peer: small_tile.at[me_t], small_tile.at[me_t], st_send, st_recv)

    def later_rows(block):
        spread_rows(block + spread_blocks // 2)
    rows_loop(spread_blocks - spread_blocks // 2, later_rows)

    def edge_row(p):
        for d in range(H):
            at = d * ts + p
            rimf[0, pl.ds(at, 1), :] = gpad[H - 1 - d, pl.ds(H + ts - 1 - p, 1), :]
            rimf[0, pl.ds(strip + at, 1), :] = gpad[H + ts - 1 - p, H + ts + d:H + ts + d + 1, :]
            rimf[1, pl.ds(strip + at, 1), :] = gpad[H + p, H - 1 - d:H - d, :]
    rows_loop(ts, edge_row)
    for c in range(2):
        rimf[c, 2 * strip:, :] = jnp.zeros((32, channels), F32)
    for d in range(H):
        rimf[1, d * ts:(d + 1) * ts, :] = gpad[H + ts + d, H:H + ts, :]
    for i in range(H):
        for j in range(H):
            spots = (
                (H - 1 - i, H + ts + H - 1 - j), (H + ts + i, H + ts + j),
                (H + ts + i, j), (H - 1 - i, H - 1 - j),
            )
            for k in range(4):
                at = 2 * strip + 16 * (k % 2) + H * i + j
                row, col = spots[k]
                rimf[k // 2, at:at + 1, :] = gpad[row, col:col + 1, :]
    rims[me_t] = rimf[...].astype(BF16)
    rim_copies = to_peers("tile", tiles, me_t, lambda peer: rims.at[me_t, me_c], rims.at[me_t, me_c], rim_send, rim_recv)

    def base_row(i):
        base[i] = ct_ref[i].astype(F32) + gpad[H + i, H:H + ts, :]
    rows_loop(ts, base_row)

    for copy in rs_copies:
        copy.wait_recv()
    total = piece_recv[0].astype(F32)
    for t in range(1, tiles):
        total = total + piece_recv[t].astype(F32)
    piece_all[me_t] = (total * factor).astype(BF16)
    tg_copies = to_peers("tile", tiles, me_t, lambda peer: piece_all.at[me_t], piece_all.at[me_t], tg_send, tg_recv)
    for copy in st_copies:
        copy.wait_recv()
    total = small_tile[0]
    for t in range(1, tiles):
        total = total + small_tile[t]
    small_done[me_c] = total * factor
    done_copy = to_sibling(small_done.at[me_c], small_done.at[me_c], 5)

    rim_passes = []
    for o in range(1, tiles):
        rim_copies[o - 1].wait_recv()
        source = lax.rem(me_t - o + tiles, tiles)
        rim_passes.append(to_sibling(rims.at[source, me_c], rims.at[source, me_c], 5 + tiles - 1 + o))
    for copy in rim_passes:
        copy.wait_recv()
    for f in range(4):
        def gather(p, carry):
            edge, at_start, at_end = carry
            for k in range(8):
                face = (adj[p, k, 1] + facing_turns[k]) % 4
                chosen = jnp.where((adj[p, k, 0] == me_t) & (face == f), 1.0, 0.0).astype(F32)
                if k < 4:
                    edge = edge + chosen * rims[p, k // 2, strip * (k % 2):strip * (k % 2 + 1), :].astype(F32)
                else:
                    at = 2 * strip + 16 * (k % 2)
                    piece = chosen * rims[p, (k - 4) // 2, at:at + 16, :].astype(F32)
                    if corner_at_end[k - 4]:
                        at_end = at_end + piece
                    else:
                        at_start = at_start + piece
            return edge, at_start, at_end
        zero = jnp.zeros((16, channels), F32)
        edge, at_start, at_end = lax.fori_loop(0, tiles, gather, (jnp.zeros((strip, channels), F32), zero, zero))
        incoming[f] = edge
        for d in range(H):
            incoming[f, d * ts:d * ts + H, :] += at_start[d * H:(d + 1) * H]
            incoming[f, (d + 1) * ts - H:(d + 1) * ts, :] += at_end[d * H:(d + 1) * H]
    for d in range(H):
        base[d] += incoming[0, d * ts:(d + 1) * ts, :]

    def add_row(p):
        for d in range(H):
            base[p, ts - H + d:ts - H + d + 1, :] += incoming[1, pl.ds((H - 1 - d) * ts + p, 1), :]
            base[ts - H + d, pl.ds(p, 1), :] += incoming[2, pl.ds((H - 1 - d) * ts + ts - 1 - p, 1), :]
            base[p, d:d + 1, :] += incoming[3, pl.ds(d * ts + ts - 1 - p, 1), :]
    rows_loop(ts, add_row)

    def out_row(i):
        out_ref[i] = base[i].astype(BF16)
    rows_loop(ts, out_row)

    for copy in tg_copies:
        copy.wait_recv()
    for t in range(tiles):
        w_out_all[t * piece_rows:(t + 1) * piece_rows, :] = piece_all[t].astype(F32)
    done_copy.wait_recv()
    small_out[...] = small_done[...]

    for copy in face_copies + face_passes + rim_copies + rim_passes + rs_copies + dp_copies + sd_copies + tg_copies + st_copies + [
        win_copy, wout_copy, cg_copy, part_copy, small_copy, done_copy
    ]:
        copy.wait_send()


def on_device(inputs, kernel, norm_gain, w_in, w_out, layer_scale, cotangent, adjacency):
    ts, ch = inputs.shape[2], inputs.shape[4]
    hid = w_in.shape[1]
    tiles, dps = lax.axis_size("tile"), lax.axis_size("dp")
    factor = 1.0 / math.sqrt(dps * tiles * ts * ts)
    strip = H * ts
    rim_rows = 2 * strip + 32
    piece = 2 * (ch // dps) // tiles
    half_small = SMALL_ROWS // 2
    part_rows = ch // dps
    vmem = pl.BlockSpec(memory_space=pltpu.VMEM)
    hbm = pl.BlockSpec(memory_space=pltpu.MemorySpace.HBM)
    dma = pltpu.SemaphoreType.DMA
    peers_t, peers_d = max(tiles - 1, 1), max(dps - 1, 1)
    out, small, grads = pl.pallas_call(
        functools.partial(body, tiles, dps, factor),
        out_shape=(
            jax.ShapeDtypeStruct((ts, ts, ch), BF16),
            jax.ShapeDtypeStruct((2, SMALL_ROWS // 2, ch), F32),
            jax.ShapeDtypeStruct((2 * part_rows, hid), F32),
        ),
        in_specs=[pl.BlockSpec(memory_space=pltpu.SMEM), hbm, hbm, vmem, vmem, hbm, hbm, vmem],
        out_specs=(vmem,) * 3,
        scratch_shapes=[
            pltpu.VMEM((ts + 2 * H, ts + 2 * COL, ch), F32),
            pltpu.VMEM((8, strip, ch), F32),
            pltpu.VMEM((tiles, 4, strip, ch), BF16),
            pltpu.VMEM((2, ch, hid), BF16),
            pltpu.VMEM((2, hid, ch), BF16),
            pltpu.VMEM((ts // 2, ts, ch), F32),
            pltpu.VMEM((2, 2, ch, hid), F32),
            pltpu.VMEM((ts, ts, ch), BF16),
            pltpu.VMEM((ts + 2 * (KS - 1), ts + 2 * COL, ch), F32),
            pltpu.VMEM((ts + 2 * H, ts + 8, ch), F32),
            pltpu.VMEM((2, rim_rows, ch), F32),
            pltpu.VMEM((tiles, 2, rim_rows, ch), BF16),
            pltpu.VMEM((4, strip, ch), F32),
            pltpu.VMEM((2, ch, hid), F32),
            pltpu.VMEM((dps, 2, part_rows, hid), F32),
            pltpu.VMEM((dps, 2, part_rows, hid), F32),
            pltpu.VMEM((tiles, piece, hid), BF16),
            pltpu.VMEM((tiles, piece, hid), BF16),
            pltpu.VMEM((tiles, piece, hid), BF16),
            pltpu.VMEM((SMALL_ROWS, 8, ch), F32),
            pltpu.VMEM((2, half_small, ch), F32),
            pltpu.VMEM((half_small, ch), F32),
            pltpu.VMEM((dps, half_small, ch), F32),
            pltpu.VMEM((tiles, half_small, ch), F32),
            pltpu.VMEM((2, half_small, ch), F32),
            pltpu.VMEM((ts, ts, ch), F32),
            pltpu.VMEM((ts, ts, ch), BF16),
            pltpu.VMEM((ts, ts, ch), BF16),
            dma((4,)),
            dma((peers_t,)), dma((peers_t,)), dma((4 + 2 * tiles,)), dma((4 + 2 * tiles,)), dma((peers_t,)), dma((peers_t,)),
            dma((peers_d,)), dma((peers_d,)), dma((peers_t,)), dma((peers_t,)), dma((peers_t,)), dma((peers_t,)),
            dma((peers_d,)), dma((peers_d,)), dma((peers_t,)), dma((peers_t,)),
        ],
        compiler_params=pltpu.CompilerParams(
            collective_id=0, has_side_effects=True, vmem_limit_bytes=64 * 1024 * 1024 - 64 * 1024
        ),
    )(
        adjacency, inputs[0, 0], cotangent[0, 0], kernel, norm_gain[None], w_in, w_out, layer_scale[None]
    )
    taps = KS * KS
    small = small.reshape(SMALL_ROWS, ch)
    return (
        out[None, None],
        small[:taps],
        small[taps],
        grads[:part_rows],
        grads[part_rows:].T,
        small[taps + 1],
    )


def solution(mesh):
    placed = (
        P(("group", "dp"), "tile", None, None, None),
        P(),
        P(),
        P(None, "chan"),
        P("chan", None),
        P(),
        P(("group", "dp"), "tile", None, None, None),
        P(),
    )
    return jax.shard_map(
        on_device,
        mesh=mesh,
        in_specs=placed,
        out_specs=(
            P(("group", "dp"), "tile", None, None, None),
            P("group", None),
            P("group"),
            P(("group", "dp"), "chan"),
            P(("group", "chan"), "dp"),
            P("group"),
        ),
        check_vma=False,
    )
```

```python
import functools
import math

import jax
import jax.numpy as jnp
from jax import lax
from jax.experimental import pallas as pl
from jax.experimental.pallas import tpu as pltpu
from jax.sharding import PartitionSpec as P

KS = 7
H = KS // 2
COL = 8
ROWS_AT_ONCE = 4
SMALL_ROWS = 64

eps = 1e-06
root_two_pi = 0.7978845608028654
cubic_coef = 0.044715
facing_turns = (2, 3, 0, 1, 2, 0, 0, 2)
corner_at_end = (True, False, True, False)
MESH = pl.DeviceIdType.MESH
F32 = jnp.float32
BF16 = jnp.bfloat16


def gelu_pair(values):
    square = values * values
    tanh_part = jnp.tanh(values * (root_two_pi + (root_two_pi * cubic_coef) * square))
    half_up = 0.5 + 0.5 * tanh_part
    active = values * half_up
    gelu_slope = half_up + active * (1.0 - tanh_part) * (
        root_two_pi + (3.0 * root_two_pi * cubic_coef) * square
    )
    return active, gelu_slope


def mm(left, right, left_dim, right_dim):
    return lax.dot_general(
        left, right, (((left_dim,), (right_dim,)), ((), ())), preferred_element_type=F32
    )


def body(
    tiles, dps, factor,
    adj, x_hbm, ct_hbm, kern, gain_ref, w_in_ref, w_out_ref, scale_ref,
    out_ref, small_out, w_out_all,
    pad, strips, faces, win, wout, conv_ref, part, cg, cpad, gpad, rimf, rims, incoming,
    chan_recv, dp_send, dp_recv, piece_send, piece_recv, piece_all, kacc, small_part, small_recv,
    small_dp, small_tile, small_done, base, x_ref, ct_ref, local_sem,
    face_send, face_recv, pair_send, pair_recv, rim_send, rim_recv,
    dp_send_sem, dp_recv_sem, rs_send, rs_recv, tg_send, tg_recv, sd_send, sd_recv, st_send, st_recv,
):
    ts = x_ref.shape[0]
    half = ts // 2
    strip = H * ts
    me_t = lax.axis_index("tile")
    me_d = lax.axis_index("dp")
    me_c = lax.axis_index("chan")
    sib = 1 - me_c

    x_copy = pltpu.make_async_copy(x_hbm, x_ref, local_sem.at[0])
    x_copy.start()
    win_local = pltpu.make_async_copy(w_in_ref, win.at[me_c], local_sem.at[1])
    win_local.start()
    wout_local = pltpu.make_async_copy(w_out_ref, wout.at[me_c], local_sem.at[2])
    wout_local.start()
    ct_copy = pltpu.make_async_copy(ct_hbm, ct_ref, local_sem.at[3])
    ct_copy.start()

    barrier = pltpu.get_barrier_semaphore()
    for o in range(1, tiles):
        pl.semaphore_signal(barrier, inc=1, device_id={"tile": lax.rem(me_t + o, tiles)}, device_id_type=MESH)
    for o in range(1, dps):
        pl.semaphore_signal(barrier, inc=1, device_id={"dp": lax.rem(me_d + o, dps)}, device_id_type=MESH)
    pl.semaphore_signal(barrier, inc=1, device_id={"chan": sib}, device_id_type=MESH)

    def to_peers(axis, size, me, source, target, send_sems, recv_sems):
        copies = []
        for o in range(1, size):
            peer = lax.rem(me + o, size)
            copy = pltpu.make_async_remote_copy(
                src_ref=source(peer), dst_ref=target, send_sem=send_sems.at[o - 1],
                recv_sem=recv_sems.at[o - 1], device_id={axis: peer}, device_id_type=MESH,
            )
            copy.start()
            copies.append(copy)
        return copies

    def to_sibling(source, target, index):
        copy = pltpu.make_async_remote_copy(
            src_ref=source, dst_ref=target, send_sem=pair_send.at[index],
            recv_sem=pair_recv.at[index], device_id={"chan": sib}, device_id_type=MESH,
        )
        copy.start()
        return copy

    def rows_loop(count, step):
        def wrapped(index, carry):
            step(index)
            return carry
        lax.fori_loop(0, count, wrapped, 0)

    x_copy.wait()

    def fill(i):
        pad[H + i, COL:COL + ts, :] = x_ref[i].astype(F32)
    rows_loop(ts, fill)
    for d in range(H):
        strips[0, d * ts:(d + 1) * ts, :] = x_ref[d].astype(F32)

    def face_row(p):
        for d in range(H):
            strips[1, pl.ds(d * ts + p, 1), :] = pad[H + p, COL + ts - 1 - d:COL + ts - d, :]
            strips[2, pl.ds(d * ts + p, 1), :] = pad[H + ts - 1 - d, pl.ds(COL + ts - 1 - p, 1), :]
            strips[3, pl.ds(d * ts + p, 1), :] = pad[H + ts - 1 - p, COL + d:COL + d + 1, :]
    rows_loop(ts, face_row)
    for f in range(4):
        faces[me_t, f] = strips[f].astype(BF16)

    pl.semaphore_wait(barrier, tiles - 1 + dps - 1 + 1)
    mine = pl.ds(2 * me_c, 2)
    face_copies = to_peers("tile", tiles, me_t, lambda peer: faces.at[me_t, mine], faces.at[me_t, mine], face_send, face_recv)
    win_copy = to_sibling(w_in_ref, win.at[me_c], 0)
    wout_copy = to_sibling(w_out_ref, wout.at[me_c], 1)

    def zero_rows(i):
        cpad[i] = jnp.zeros(cpad.shape[1:], F32)
    rows_loop(cpad.shape[0], zero_rows)
    kacc[...] = jnp.zeros_like(kacc)

    face_passes = []
    for o in range(1, tiles):
        face_copies[o - 1].wait_recv()
        source = lax.rem(me_t - o + tiles, tiles)
        face_passes.append(to_sibling(faces.at[source, mine], faces.at[source, mine], 5 + o))
    for copy in face_passes:
        copy.wait_recv()

    for k in range(8):
        source = adj[me_t, 0, k]
        face = (adj[me_t, 1, k] + facing_turns[k]) % 4
        strips[k] = faces[source, face].astype(F32)
    for d in range(H):
        pad[H + ts + d, COL:COL + ts, :] = strips[2, d * ts:(d + 1) * ts, :]

    def rim_row(p):
        for d in range(H):
            pad[d, pl.ds(COL + p, 1), :] = strips[0, pl.ds((H - 1 - d) * ts + ts - 1 - p, 1), :]
            pad[H + p, COL + ts + d:COL + ts + d + 1, :] = strips[1, pl.ds(d * ts + ts - 1 - p, 1), :]
            pad[H + p, COL - H + d:COL - H + d + 1, :] = strips[3, pl.ds((H - 1 - d) * ts + p, 1), :]
    rows_loop(ts, rim_row)
    for i in range(H):
        for j in range(H):
            at = (H - 1 - i) * ts + ts - H + (H - 1 - j)
            pad[i, COL + ts + j:COL + ts + j + 1, :] = strips[4, at:at + 1, :]
            at = i * ts + j
            pad[H + ts + i, COL + ts + j:COL + ts + j + 1, :] = strips[5, at:at + 1, :]
            at = i * ts + ts - H + j
            pad[H + ts + i, COL - H + j:COL - H + j + 1, :] = strips[6, at:at + 1, :]
            at = (H - 1 - i) * ts + (H - 1 - j)
            pad[i, COL - H + j:COL - H + j + 1, :] = strips[7, at:at + 1, :]

    first = me_c * half

    def conv_rows(block):
        i = block * ROWS_AT_ONCE
        acc = [jnp.zeros((ts, pad.shape[2]), F32) for _ in range(ROWS_AT_ONCE)]
        for a in range(ROWS_AT_ONCE + KS - 1):
            for b in range(KS):
                window = pad[first + i + a, COL - H + b:COL - H + b + ts, :]
                for r in range(ROWS_AT_ONCE):
                    if 0 <= a - r < KS:
                        at = (a - r) * KS + b
                        acc[r] = acc[r] + window * kern[at:at + 1, :]
        for r in range(ROWS_AT_ONCE):
            conv_ref[i + r] = acc[r]
    rows_loop(half // ROWS_AT_ONCE, conv_rows)

    win_copy.wait_recv()
    wout_copy.wait_recv()
    win_local.wait()
    wout_local.wait()
    ct_copy.wait()

    gain = gain_ref[...]
    layer_scale = scale_ref[...]
    block_rows = 8
    pixels = block_rows * ts
    channels = pad.shape[2]
    gain_total = jnp.zeros((1, channels), F32)
    scale_total = jnp.zeros((1, channels), F32)
    for block in range(half // block_rows):
        at = block * block_rows
        conv = conv_ref[at:at + block_rows].reshape(pixels, channels)
        mean = jnp.mean(conv, axis=1, keepdims=True)
        centred = conv - mean
        inv_std = lax.rsqrt(jnp.mean(centred * centred, axis=1, keepdims=True) + eps)
        normed = centred * inv_std
        normed_b = (normed * gain).astype(BF16)
        upstream = ct_ref[pl.ds(first + at, block_rows)].reshape(pixels, channels).astype(F32)
        scaled_b = (upstream * layer_scale).astype(BF16)
        branch = jnp.zeros((pixels, channels), F32)
        normed_grad = jnp.zeros((pixels, channels), F32)
        for c in range(2):
            active, slope = gelu_pair(mm(normed_b, win[c], 1, 0))
            active_b = active.astype(BF16)
            branch = branch + mm(active_b, wout[c], 1, 0)
            hidden_grad = (mm(scaled_b, wout[c], 1, 1) * slope).astype(BF16)
            normed_grad = normed_grad + mm(hidden_grad, win[c], 1, 1)
            in_grad = mm(normed_b, hidden_grad, 0, 0)
            out_grad = mm(scaled_b, active_b, 0, 0)
            if block == 0:
                part[c, 0] = in_grad
                part[c, 1] = out_grad
            else:
                part[c, 0] += in_grad
                part[c, 1] += out_grad
        scale_total = scale_total + jnp.sum(upstream * branch, axis=0, keepdims=True)
        gain_total = gain_total + jnp.sum(normed_grad * normed, axis=0, keepdims=True)
        scaled = normed_grad * gain
        first_mean = jnp.mean(scaled, axis=1, keepdims=True)
        second_mean = jnp.mean(scaled * normed, axis=1, keepdims=True)
        grad_b = (inv_std * (scaled - first_mean - normed * second_mean)).astype(BF16)
        cg[pl.ds(first + at, block_rows)] = grad_b.reshape(block_rows, ts, channels)

    cg_copy = to_sibling(cg.at[pl.ds(first, half)], cg.at[pl.ds(first, half)], 2)
    part_copy = to_sibling(part.at[sib], chan_recv, 3)

    for a in range(KS):
        def kernel_row(i, acc):
            grad = cg[first + i].astype(F32)
            new = []
            for b in range(KS):
                window = pad[first + i + a, COL - H + b:COL - H + b + ts, :]
                new.append(acc[b] + jnp.sum((window * grad).reshape(ts // 8, 8, channels), axis=0))
            return tuple(new)
        sums = lax.fori_loop(0, half, kernel_row, tuple(jnp.zeros((8, channels), F32) for _ in range(KS)))
        for b in range(KS):
            kacc[a * KS + b] = sums[b]
    for c in range(2):
        small_part[c] = jnp.sum(kacc[c * SMALL_ROWS // 2:(c + 1) * SMALL_ROWS // 2], axis=1)
    at = KS * KS - SMALL_ROWS // 2
    small_part[1, at:at + 1, :] = gain_total
    small_part[1, at + 1:at + 2, :] = scale_total
    small_copy = to_sibling(small_part.at[sib], small_recv, 4)

    cg_copy.wait_recv()

    def widen(i):
        cpad[KS - 1 + i, COL:COL + ts, :] = cg[i].astype(F32)
    rows_loop(ts, widen)
    wide = gpad.shape[1]

    def spread_rows(block):
        i = block * 2
        acc = [jnp.zeros((wide, channels), F32) for _ in range(2)]
        for a in range(KS + 1):
            for b in range(KS):
                window = cpad[i + a, COL - (KS - 1) + b:COL - (KS - 1) + b + wide, :]
                for r in range(2):
                    if 0 <= a - r < KS:
                        at = (KS - 1 - (a - r)) * KS + KS - 1 - b
                        acc[r] = acc[r] + window * kern[at:at + 1, :]
        for r in range(2):
            gpad[i + r] = acc[r]
    spread_blocks = (ts + 2 * H) // 2
    rows_loop(spread_blocks // 2, spread_rows)

    part_rows = channels // dps
    part_copy.wait_recv()
    for w in range(2):
        for d in range(dps):
            rows = slice(d * part_rows, (d + 1) * part_rows)
            dp_send[d, w] = part[me_c, w, rows, :] + chan_recv[w, rows, :]
    dp_recv[me_d] = dp_send[me_d]
    dp_copies = to_peers("dp", dps, me_d, lambda peer: dp_send.at[peer], dp_recv.at[me_d], dp_send_sem, dp_recv_sem)
    small_copy.wait_recv()
    small_dp[me_d] = small_part[me_c] + small_recv[...]
    sd_copies = to_peers("dp", dps, me_d, lambda peer: small_dp.at[me_d], small_dp.at[me_d], sd_send, sd_recv)

    def later_rows(block):
        spread_rows(block + spread_blocks // 2)
    rows_loop(spread_blocks - spread_blocks // 2, later_rows)

    def edge_row(p):
        for d in range(H):
            at = d * ts + p
            rimf[0, pl.ds(at, 1), :] = gpad[H - 1 - d, pl.ds(H + ts - 1 - p, 1), :]
            rimf[0, pl.ds(strip + at, 1), :] = gpad[H + ts - 1 - p, H + ts + d:H + ts + d + 1, :]
            rimf[1, pl.ds(strip + at, 1), :] = gpad[H + p, H - 1 - d:H - d, :]
    rows_loop(ts, edge_row)
    for c in range(2):
        rimf[c, 2 * strip:, :] = jnp.zeros((32, channels), F32)
    for d in range(H):
        rimf[1, d * ts:(d + 1) * ts, :] = gpad[H + ts + d, H:H + ts, :]
    for i in range(H):
        for j in range(H):
            spots = (
                (H - 1 - i, H + ts + H - 1 - j), (H + ts + i, H + ts + j),
                (H + ts + i, j), (H - 1 - i, H - 1 - j),
            )
            for k in range(4):
                at = 2 * strip + 16 * (k % 2) + H * i + j
                row, col = spots[k]
                rimf[k // 2, at:at + 1, :] = gpad[row, col:col + 1, :]
    rims[me_t] = rimf[...].astype(BF16)
    rim_copies = to_peers("tile", tiles, me_t, lambda peer: rims.at[me_t, me_c], rims.at[me_t, me_c], rim_send, rim_recv)

    piece_rows = 2 * part_rows // tiles
    for copy in dp_copies:
        copy.wait_recv()
    total = dp_recv[0]
    for d in range(1, dps):
        total = total + dp_recv[d]
    total = total.reshape(2 * part_rows, total.shape[2]).astype(BF16)
    for t in range(tiles):
        piece_send[t] = total[t * piece_rows:(t + 1) * piece_rows]
    piece_recv[me_t] = piece_send[me_t]
    rs_copies = to_peers("tile", tiles, me_t, lambda peer: piece_send.at[peer], piece_recv.at[me_t], rs_send, rs_recv)
    for copy in sd_copies:
        copy.wait_recv()
    total = small_dp[0]
    for d in range(1, dps):
        total = total + small_dp[d]
    small_tile[me_t] = total
    st_copies = to_peers("tile", tiles, me_t, lambda peer: small_tile.at[me_t], small_tile.at[me_t], st_send, st_recv)

    def base_row(i):
        base[i] = ct_ref[i].astype(F32) + gpad[H + i, H:H + ts, :]
    rows_loop(ts, base_row)

    for copy in rs_copies:
        copy.wait_recv()
    total = piece_recv[0].astype(F32)
    for t in range(1, tiles):
        total = total + piece_recv[t].astype(F32)
    piece_all[me_t] = (total * factor).astype(BF16)
    tg_copies = to_peers("tile", tiles, me_t, lambda peer: piece_all.at[me_t], piece_all.at[me_t], tg_send, tg_recv)
    for copy in st_copies:
        copy.wait_recv()
    total = small_tile[0]
    for t in range(1, tiles):
        total = total + small_tile[t]
    small_done[me_c] = total * factor
    done_copy = to_sibling(small_done.at[me_c], small_done.at[me_c], 5)

    rim_passes = []
    for o in range(1, tiles):
        rim_copies[o - 1].wait_recv()
        source = lax.rem(me_t - o + tiles, tiles)
        rim_passes.append(to_sibling(rims.at[source, me_c], rims.at[source, me_c], 5 + tiles - 1 + o))
    for copy in rim_passes:
        copy.wait_recv()
    for f in range(4):
        def gather(p, carry):
            edge, at_start, at_end = carry
            for k in range(8):
                face = (adj[p, 1, k] + facing_turns[k]) % 4
                chosen = jnp.where((adj[p, 0, k] == me_t) & (face == f), 1.0, 0.0).astype(F32)
                if k < 4:
                    edge = edge + chosen * rims[p, k // 2, strip * (k % 2):strip * (k % 2 + 1), :].astype(F32)
                else:
                    at = 2 * strip + 16 * (k % 2)
                    piece = chosen * rims[p, (k - 4) // 2, at:at + 16, :].astype(F32)
                    if corner_at_end[k - 4]:
                        at_end = at_end + piece
                    else:
                        at_start = at_start + piece
            return edge, at_start, at_end
        zero = jnp.zeros((16, channels), F32)
        edge, at_start, at_end = lax.fori_loop(0, tiles, gather, (jnp.zeros((strip, channels), F32), zero, zero))
        incoming[f] = edge
        for d in range(H):
            incoming[f, d * ts:d * ts + H, :] += at_start[d * H:(d + 1) * H]
            incoming[f, (d + 1) * ts - H:(d + 1) * ts, :] += at_end[d * H:(d + 1) * H]
    for d in range(H):
        base[d] += incoming[0, d * ts:(d + 1) * ts, :]

    def add_row(p):
        for d in range(H):
            base[p, ts - H + d:ts - H + d + 1, :] += incoming[1, pl.ds((H - 1 - d) * ts + p, 1), :]
            base[ts - H + d, pl.ds(p, 1), :] += incoming[2, pl.ds((H - 1 - d) * ts + ts - 1 - p, 1), :]
            base[p, d:d + 1, :] += incoming[3, pl.ds(d * ts + ts - 1 - p, 1), :]
    rows_loop(ts, add_row)

    def out_row(i):
        out_ref[i] = base[i].astype(BF16)
    rows_loop(ts, out_row)

    for copy in tg_copies:
        copy.wait_recv()
    for t in range(tiles):
        w_out_all[t * piece_rows:(t + 1) * piece_rows, :] = piece_all[t].astype(F32)
    done_copy.wait_recv()
    small_out[...] = small_done[...]

    for copy in face_copies + face_passes + rim_copies + rim_passes + rs_copies + dp_copies + sd_copies + tg_copies + st_copies + [
        win_copy, wout_copy, cg_copy, part_copy, small_copy, done_copy
    ]:
        copy.wait_send()


def in_hbm(array):
    return pltpu.with_memory_space_constraint(array, pltpu.MemorySpace.HBM)


def on_device(inputs, kernel, norm_gain, w_in, w_out, layer_scale, cotangent, adjacency):
    ts, ch = inputs.shape[2], inputs.shape[4]
    hid = w_in.shape[1]
    tiles, dps = lax.axis_size("tile"), lax.axis_size("dp")
    factor = 1.0 / math.sqrt(dps * tiles * ts * ts)
    strip = H * ts
    rim_rows = 2 * strip + 32
    piece = 2 * (ch // dps) // tiles
    half_small = SMALL_ROWS // 2
    part_rows = ch // dps
    vmem = pl.BlockSpec(memory_space=pltpu.VMEM)
    hbm = pl.BlockSpec(memory_space=pltpu.MemorySpace.HBM)
    dma = pltpu.SemaphoreType.DMA
    peers_t, peers_d = max(tiles - 1, 1), max(dps - 1, 1)
    out, small, grads = pl.pallas_call(
        functools.partial(body, tiles, dps, factor),
        out_shape=(
            jax.ShapeDtypeStruct((ts, ts, ch), BF16),
            jax.ShapeDtypeStruct((2, SMALL_ROWS // 2, ch), F32),
            jax.ShapeDtypeStruct((2 * part_rows, hid), F32),
        ),
        in_specs=[pl.BlockSpec(memory_space=pltpu.SMEM), hbm, hbm, vmem, vmem, hbm, hbm, vmem],
        out_specs=(vmem,) * 3,
        scratch_shapes=[
            pltpu.VMEM((ts + 2 * H, ts + 2 * COL, ch), F32),
            pltpu.VMEM((8, strip, ch), F32),
            pltpu.VMEM((tiles, 4, strip, ch), BF16),
            pltpu.VMEM((2, ch, hid), BF16),
            pltpu.VMEM((2, hid, ch), BF16),
            pltpu.VMEM((ts // 2, ts, ch), F32),
            pltpu.VMEM((2, 2, ch, hid), F32),
            pltpu.VMEM((ts, ts, ch), BF16),
            pltpu.VMEM((ts + 2 * (KS - 1), ts + 2 * COL, ch), F32),
            pltpu.VMEM((ts + 2 * H, ts + 8, ch), F32),
            pltpu.VMEM((2, rim_rows, ch), F32),
            pltpu.VMEM((tiles, 2, rim_rows, ch), BF16),
            pltpu.VMEM((4, strip, ch), F32),
            pltpu.VMEM((2, ch, hid), F32),
            pltpu.VMEM((dps, 2, part_rows, hid), F32),
            pltpu.VMEM((dps, 2, part_rows, hid), F32),
            pltpu.VMEM((tiles, piece, hid), BF16),
            pltpu.VMEM((tiles, piece, hid), BF16),
            pltpu.VMEM((tiles, piece, hid), BF16),
            pltpu.VMEM((SMALL_ROWS, 8, ch), F32),
            pltpu.VMEM((2, half_small, ch), F32),
            pltpu.VMEM((half_small, ch), F32),
            pltpu.VMEM((dps, half_small, ch), F32),
            pltpu.VMEM((tiles, half_small, ch), F32),
            pltpu.VMEM((2, half_small, ch), F32),
            pltpu.VMEM((ts, ts, ch), F32),
            pltpu.VMEM((ts, ts, ch), BF16),
            pltpu.VMEM((ts, ts, ch), BF16),
            dma((4,)),
            dma((peers_t,)), dma((peers_t,)), dma((4 + 2 * tiles,)), dma((4 + 2 * tiles,)), dma((peers_t,)), dma((peers_t,)),
            dma((peers_d,)), dma((peers_d,)), dma((peers_t,)), dma((peers_t,)), dma((peers_t,)), dma((peers_t,)),
            dma((peers_d,)), dma((peers_d,)), dma((peers_t,)), dma((peers_t,)),
        ],
        compiler_params=pltpu.CompilerParams(
            collective_id=0, has_side_effects=True, vmem_limit_bytes=48 * 1024 * 1024
        ),
    )(
        jnp.transpose(adjacency, (0, 2, 1)), in_hbm(inputs[0, 0]), in_hbm(cotangent[0, 0]), kernel,
        norm_gain[None], in_hbm(w_in), in_hbm(w_out), layer_scale[None],
    )
    taps = KS * KS
    small = small.reshape(SMALL_ROWS, ch)
    return (
        out[None, None],
        small[:taps],
        small[taps],
        grads[:part_rows],
        grads[part_rows:].T,
        small[taps + 1],
    )


def solution(mesh):
    placed = (
        P(("group", "dp"), "tile", None, None, None),
        P(),
        P(),
        P(None, "chan"),
        P("chan", None),
        P(),
        P(("group", "dp"), "tile", None, None, None),
        P(),
    )
    return jax.shard_map(
        on_device,
        mesh=mesh,
        in_specs=placed,
        out_specs=(
            P(("group", "dp"), "tile", None, None, None),
            P("group", None),
            P("group"),
            P(("group", "dp"), "chan"),
            P(("group", "chan"), "dp"),
            P("group"),
        ),
        check_vma=False,
    )
```

```python
import functools
import math

import jax
import jax.numpy as jnp
from jax import lax
from jax.experimental import pallas as pl
from jax.experimental.pallas import tpu as pltpu
from jax.sharding import PartitionSpec as P

KS = 7
H = KS // 2
COL = 8
ROWS_AT_ONCE = 4
SMALL_ROWS = 64

eps = 1e-06
root_two_pi = 0.7978845608028654
cubic_coef = 0.044715
facing_turns = (2, 3, 0, 1, 2, 0, 0, 2)
corner_at_end = (True, False, True, False)
MESH = pl.DeviceIdType.MESH
F32 = jnp.float32
BF16 = jnp.bfloat16


def gelu_pair(values):
    square = values * values
    tanh_part = jnp.tanh(values * (root_two_pi + (root_two_pi * cubic_coef) * square))
    half_up = 0.5 + 0.5 * tanh_part
    active = values * half_up
    gelu_slope = half_up + active * (1.0 - tanh_part) * (
        root_two_pi + (3.0 * root_two_pi * cubic_coef) * square
    )
    return active, gelu_slope


def mm(left, right, left_dim, right_dim):
    return lax.dot_general(
        left, right, (((left_dim,), (right_dim,)), ((), ())), preferred_element_type=F32
    )


def body(
    tiles, dps, factor,
    adj, x_hbm, ct_hbm, kern, gain_ref, w_in_ref, w_out_ref, scale_ref,
    out_ref, small_out, w_out_all,
    pad, strips, faces, win, wout, conv_ref, part, cg, cpad, gpad, rimf, rims, incoming,
    chan_recv, dp_send, dp_recv, piece_send, piece_recv, piece_all, kacc, small_part, small_recv,
    small_dp, small_tile, small_done, base, x_ref, ct_ref, local_sem,
    face_send, face_recv, pair_send, pair_recv, rim_send, rim_recv,
    dp_send_sem, dp_recv_sem, rs_send, rs_recv, tg_send, tg_recv, sd_send, sd_recv, st_send, st_recv,
):
    ts = x_ref.shape[0]
    half = ts // 2
    strip = H * ts
    me_t = lax.axis_index("tile")
    me_d = lax.axis_index("dp")
    me_c = lax.axis_index("chan")
    sib = 1 - me_c

    x_copy = pltpu.make_async_copy(x_hbm, x_ref, local_sem.at[0])
    x_copy.start()
    win_local = pltpu.make_async_copy(w_in_ref, win.at[me_c], local_sem.at[1])
    win_local.start()
    wout_local = pltpu.make_async_copy(w_out_ref, wout.at[me_c], local_sem.at[2])
    wout_local.start()
    ct_copy = pltpu.make_async_copy(ct_hbm, ct_ref, local_sem.at[3])
    ct_copy.start()

    barrier = pltpu.get_barrier_semaphore()
    for o in range(1, tiles):
        pl.semaphore_signal(barrier, inc=1, device_id={"tile": lax.rem(me_t + o, tiles)}, device_id_type=MESH)
    for o in range(1, dps):
        pl.semaphore_signal(barrier, inc=1, device_id={"dp": lax.rem(me_d + o, dps)}, device_id_type=MESH)
    pl.semaphore_signal(barrier, inc=1, device_id={"chan": sib}, device_id_type=MESH)

    def to_peers(axis, size, me, source, target, send_sems, recv_sems):
        copies = []
        for o in range(1, size):
            peer = lax.rem(me + o, size)
            copy = pltpu.make_async_remote_copy(
                src_ref=source(peer), dst_ref=target, send_sem=send_sems.at[o - 1],
                recv_sem=recv_sems.at[o - 1], device_id={axis: peer}, device_id_type=MESH,
            )
            copy.start()
            copies.append(copy)
        return copies

    def to_sibling(source, target, index):
        copy = pltpu.make_async_remote_copy(
            src_ref=source, dst_ref=target, send_sem=pair_send.at[index],
            recv_sem=pair_recv.at[index], device_id={"chan": sib}, device_id_type=MESH,
        )
        copy.start()
        return copy

    def rows_loop(count, step):
        def wrapped(index, carry):
            step(index)
            return carry
        lax.fori_loop(0, count, wrapped, 0)

    x_copy.wait()

    def fill(i):
        pad[H + i, COL:COL + ts, :] = x_ref[i].astype(F32)
    rows_loop(ts, fill)
    for d in range(H):
        strips[0, d * ts:(d + 1) * ts, :] = x_ref[d].astype(F32)

    def face_row(p):
        for d in range(H):
            strips[1, pl.ds(d * ts + p, 1), :] = pad[H + p, COL + ts - 1 - d:COL + ts - d, :]
            strips[2, pl.ds(d * ts + p, 1), :] = pad[H + ts - 1 - d, pl.ds(COL + ts - 1 - p, 1), :]
            strips[3, pl.ds(d * ts + p, 1), :] = pad[H + ts - 1 - p, COL + d:COL + d + 1, :]
    rows_loop(ts, face_row)
    for f in range(4):
        faces[me_t, f] = strips[f].astype(BF16)

    pl.semaphore_wait(barrier, tiles - 1 + dps - 1 + 1)
    mine = pl.ds(2 * me_c, 2)
    face_copies = to_peers("tile", tiles, me_t, lambda peer: faces.at[me_t, mine], faces.at[me_t, mine], face_send, face_recv)
    win_copy = to_sibling(w_in_ref, win.at[me_c], 0)
    wout_copy = to_sibling(w_out_ref, wout.at[me_c], 1)

    def zero_rows(i):
        cpad[i] = jnp.zeros(cpad.shape[1:], F32)
    rows_loop(cpad.shape[0], zero_rows)
    kacc[...] = jnp.zeros_like(kacc)

    face_passes = []
    for o in range(1, tiles):
        face_copies[o - 1].wait_recv()
        source = lax.rem(me_t - o + tiles, tiles)
        face_passes.append(to_sibling(faces.at[source, mine], faces.at[source, mine], 5 + o))
    for copy in face_passes:
        copy.wait_recv()

    for k in range(8):
        source = adj[me_t, 0, k]
        face = (adj[me_t, 1, k] + facing_turns[k]) % 4
        strips[k] = faces[source, face].astype(F32)
    for d in range(H):
        pad[H + ts + d, COL:COL + ts, :] = strips[2, d * ts:(d + 1) * ts, :]

    def rim_row(p):
        for d in range(H):
            pad[d, pl.ds(COL + p, 1), :] = strips[0, pl.ds((H - 1 - d) * ts + ts - 1 - p, 1), :]
            pad[H + p, COL + ts + d:COL + ts + d + 1, :] = strips[1, pl.ds(d * ts + ts - 1 - p, 1), :]
            pad[H + p, COL - H + d:COL - H + d + 1, :] = strips[3, pl.ds((H - 1 - d) * ts + p, 1), :]
    rows_loop(ts, rim_row)
    for i in range(H):
        for j in range(H):
            at = (H - 1 - i) * ts + ts - H + (H - 1 - j)
            pad[i, COL + ts + j:COL + ts + j + 1, :] = strips[4, at:at + 1, :]
            at = i * ts + j
            pad[H + ts + i, COL + ts + j:COL + ts + j + 1, :] = strips[5, at:at + 1, :]
            at = i * ts + ts - H + j
            pad[H + ts + i, COL - H + j:COL - H + j + 1, :] = strips[6, at:at + 1, :]
            at = (H - 1 - i) * ts + (H - 1 - j)
            pad[i, COL - H + j:COL - H + j + 1, :] = strips[7, at:at + 1, :]

    first = me_c * half

    def conv_rows(block):
        i = block * ROWS_AT_ONCE
        acc = [jnp.zeros((ts, pad.shape[2]), F32) for _ in range(ROWS_AT_ONCE)]
        for a in range(ROWS_AT_ONCE + KS - 1):
            for b in range(KS):
                window = pad[first + i + a, COL - H + b:COL - H + b + ts, :]
                for r in range(ROWS_AT_ONCE):
                    if 0 <= a - r < KS:
                        at = (a - r) * KS + b
                        acc[r] = acc[r] + window * kern[at:at + 1, :]
        for r in range(ROWS_AT_ONCE):
            conv_ref[i + r] = acc[r]
    rows_loop(half // ROWS_AT_ONCE, conv_rows)

    win_copy.wait_recv()
    wout_copy.wait_recv()
    win_local.wait()
    wout_local.wait()
    ct_copy.wait()

    gain = gain_ref[...]
    layer_scale = scale_ref[...]
    block_rows = 8
    pixels = block_rows * ts
    channels = pad.shape[2]
    gain_total = jnp.zeros((1, channels), F32)
    scale_total = jnp.zeros((1, channels), F32)
    for block in range(half // block_rows):
        at = block * block_rows
        conv = conv_ref[at:at + block_rows].reshape(pixels, channels)
        mean = jnp.mean(conv, axis=1, keepdims=True)
        centred = conv - mean
        inv_std = lax.rsqrt(jnp.mean(centred * centred, axis=1, keepdims=True) + eps)
        normed = centred * inv_std
        normed_b = (normed * gain).astype(BF16)
        upstream = ct_ref[pl.ds(first + at, block_rows)].reshape(pixels, channels).astype(F32)
        scaled_b = (upstream * layer_scale).astype(BF16)
        branch = jnp.zeros((pixels, channels), F32)
        normed_grad = jnp.zeros((pixels, channels), F32)
        for c in range(2):
            active, slope = gelu_pair(mm(normed_b, win[c], 1, 0))
            active_b = active.astype(BF16)
            branch = branch + mm(active_b, wout[c], 1, 0)
            hidden_grad = (mm(scaled_b, wout[c], 1, 1) * slope).astype(BF16)
            normed_grad = normed_grad + mm(hidden_grad, win[c], 1, 1)
            in_grad = mm(normed_b, hidden_grad, 0, 0)
            out_grad = mm(scaled_b, active_b, 0, 0)
            if block == 0:
                part[c, 0] = in_grad
                part[c, 1] = out_grad
            else:
                part[c, 0] += in_grad
                part[c, 1] += out_grad
        scale_total = scale_total + jnp.sum(upstream * branch, axis=0, keepdims=True)
        gain_total = gain_total + jnp.sum(normed_grad * normed, axis=0, keepdims=True)
        scaled = normed_grad * gain
        first_mean = jnp.mean(scaled, axis=1, keepdims=True)
        second_mean = jnp.mean(scaled * normed, axis=1, keepdims=True)
        grad_b = (inv_std * (scaled - first_mean - normed * second_mean)).astype(BF16)
        cg[pl.ds(first + at, block_rows)] = grad_b.reshape(block_rows, ts, channels)

    cg_copy = to_sibling(cg.at[pl.ds(first, half)], cg.at[pl.ds(first, half)], 2)
    part_copy = to_sibling(part.at[sib], chan_recv, 3)

    for a in range(KS):
        def kernel_row(i, acc):
            grad = cg[first + i].astype(F32)
            new = []
            for b in range(KS):
                window = pad[first + i + a, COL - H + b:COL - H + b + ts, :]
                new.append(acc[b] + jnp.sum((window * grad).reshape(ts // 8, 8, channels), axis=0))
            return tuple(new)
        sums = lax.fori_loop(0, half, kernel_row, tuple(jnp.zeros((8, channels), F32) for _ in range(KS)))
        for b in range(KS):
            kacc[a * KS + b] = sums[b]
    for c in range(2):
        small_part[c] = jnp.sum(kacc[c * SMALL_ROWS // 2:(c + 1) * SMALL_ROWS // 2], axis=1)
    at = KS * KS - SMALL_ROWS // 2
    small_part[1, at:at + 1, :] = gain_total
    small_part[1, at + 1:at + 2, :] = scale_total
    small_copy = to_sibling(small_part.at[sib], small_recv, 4)

    cg_copy.wait_recv()

    def widen(i):
        cpad[KS - 1 + i, COL:COL + ts, :] = cg[i].astype(F32)
    rows_loop(ts, widen)
    wide = gpad.shape[1]

    def spread_rows(block):
        i = block * ROWS_AT_ONCE
        acc = [jnp.zeros((wide, channels), F32) for _ in range(ROWS_AT_ONCE)]
        for a in range(ROWS_AT_ONCE + KS - 1):
            for b in range(KS):
                window = cpad[i + a, COL - (KS - 1) + b:COL - (KS - 1) + b + wide, :]
                for r in range(ROWS_AT_ONCE):
                    if 0 <= a - r < KS:
                        at = (KS - 1 - (a - r)) * KS + KS - 1 - b
                        acc[r] = acc[r] + window * kern[at:at + 1, :]
        for r in range(ROWS_AT_ONCE):
            gpad[i + r] = acc[r]
    spread_blocks = gpad.shape[0] // ROWS_AT_ONCE
    rows_loop(spread_blocks // 2, spread_rows)

    part_rows = channels // dps
    part_copy.wait_recv()
    for w in range(2):
        for d in range(dps):
            rows = slice(d * part_rows, (d + 1) * part_rows)
            dp_send[d, w] = part[me_c, w, rows, :] + chan_recv[w, rows, :]
    dp_recv[me_d] = dp_send[me_d]
    dp_copies = to_peers("dp", dps, me_d, lambda peer: dp_send.at[peer], dp_recv.at[me_d], dp_send_sem, dp_recv_sem)
    small_copy.wait_recv()
    small_dp[me_d] = small_part[me_c] + small_recv[...]
    sd_copies = to_peers("dp", dps, me_d, lambda peer: small_dp.at[me_d], small_dp.at[me_d], sd_send, sd_recv)

    def later_rows(block):
        spread_rows(block + spread_blocks // 2)
    rows_loop(spread_blocks - spread_blocks // 2, later_rows)

    def edge_row(p):
        for d in range(H):
            at = d * ts + p
            rimf[0, pl.ds(at, 1), :] = gpad[H - 1 - d, pl.ds(H + ts - 1 - p, 1), :]
            rimf[0, pl.ds(strip + at, 1), :] = gpad[H + ts - 1 - p, H + ts + d:H + ts + d + 1, :]
            rimf[1, pl.ds(strip + at, 1), :] = gpad[H + p, H - 1 - d:H - d, :]
    rows_loop(ts, edge_row)
    for c in range(2):
        rimf[c, 2 * strip:, :] = jnp.zeros((32, channels), F32)
    for d in range(H):
        rimf[1, d * ts:(d + 1) * ts, :] = gpad[H + ts + d, H:H + ts, :]
    for i in range(H):
        for j in range(H):
            spots = (
                (H - 1 - i, H + ts + H - 1 - j), (H + ts + i, H + ts + j),
                (H + ts + i, j), (H - 1 - i, H - 1 - j),
            )
            for k in range(4):
                at = 2 * strip + 16 * (k % 2) + H * i + j
                row, col = spots[k]
                rimf[k // 2, at:at + 1, :] = gpad[row, col:col + 1, :]
    rims[me_t] = rimf[...].astype(BF16)
    rim_copies = to_peers("tile", tiles, me_t, lambda peer: rims.at[me_t, me_c], rims.at[me_t, me_c], rim_send, rim_recv)

    piece_rows = 2 * part_rows // tiles
    for copy in dp_copies:
        copy.wait_recv()
    total = dp_recv[0]
    for d in range(1, dps):
        total = total + dp_recv[d]
    total = total.reshape(2 * part_rows, total.shape[2]).astype(BF16)
    for t in range(tiles):
        piece_send[t] = total[t * piece_rows:(t + 1) * piece_rows]
    piece_recv[me_t] = piece_send[me_t]
    rs_copies = to_peers("tile", tiles, me_t, lambda peer: piece_send.at[peer], piece_recv.at[me_t], rs_send, rs_recv)
    for copy in sd_copies:
        copy.wait_recv()
    total = small_dp[0]
    for d in range(1, dps):
        total = total + small_dp[d]
    small_tile[me_t] = total
    st_copies = to_peers("tile", tiles, me_t, lambda peer: small_tile.at[me_t], small_tile.at[me_t], st_send, st_recv)

    def base_row(i):
        base[i] = ct_ref[i].astype(F32) + gpad[H + i, H:H + ts, :]
    rows_loop(ts, base_row)

    for copy in rs_copies:
        copy.wait_recv()
    total = piece_recv[0].astype(F32)
    for t in range(1, tiles):
        total = total + piece_recv[t].astype(F32)
    piece_all[me_t] = (total * factor).astype(BF16)
    tg_copies = to_peers("tile", tiles, me_t, lambda peer: piece_all.at[me_t], piece_all.at[me_t], tg_send, tg_recv)
    for copy in st_copies:
        copy.wait_recv()
    total = small_tile[0]
    for t in range(1, tiles):
        total = total + small_tile[t]
    small_done[me_c] = total * factor
    done_copy = to_sibling(small_done.at[me_c], small_done.at[me_c], 5)

    rim_passes = []
    for o in range(1, tiles):
        rim_copies[o - 1].wait_recv()
        source = lax.rem(me_t - o + tiles, tiles)
        rim_passes.append(to_sibling(rims.at[source, me_c], rims.at[source, me_c], 5 + tiles - 1 + o))
    for copy in rim_passes:
        copy.wait_recv()
    for f in range(4):
        def gather(p, carry):
            edge, at_start, at_end = carry
            for k in range(8):
                face = (adj[p, 1, k] + facing_turns[k]) % 4
                chosen = jnp.where((adj[p, 0, k] == me_t) & (face == f), 1.0, 0.0).astype(F32)
                if k < 4:
                    edge = edge + chosen * rims[p, k // 2, strip * (k % 2):strip * (k % 2 + 1), :].astype(F32)
                else:
                    at = 2 * strip + 16 * (k % 2)
                    piece = chosen * rims[p, (k - 4) // 2, at:at + 16, :].astype(F32)
                    if corner_at_end[k - 4]:
                        at_end = at_end + piece
                    else:
                        at_start = at_start + piece
            return edge, at_start, at_end
        zero = jnp.zeros((16, channels), F32)
        edge, at_start, at_end = lax.fori_loop(0, tiles, gather, (jnp.zeros((strip, channels), F32), zero, zero))
        incoming[f] = edge
        for d in range(H):
            incoming[f, d * ts:d * ts + H, :] += at_start[d * H:(d + 1) * H]
            incoming[f, (d + 1) * ts - H:(d + 1) * ts, :] += at_end[d * H:(d + 1) * H]
    for d in range(H):
        base[d] += incoming[0, d * ts:(d + 1) * ts, :]

    def add_row(p):
        for d in range(H):
            base[p, ts - H + d:ts - H + d + 1, :] += incoming[1, pl.ds((H - 1 - d) * ts + p, 1), :]
            base[ts - H + d, pl.ds(p, 1), :] += incoming[2, pl.ds((H - 1 - d) * ts + ts - 1 - p, 1), :]
            base[p, d:d + 1, :] += incoming[3, pl.ds(d * ts + ts - 1 - p, 1), :]
    rows_loop(ts, add_row)

    def out_row(i):
        out_ref[i] = base[i].astype(BF16)
    rows_loop(ts, out_row)

    for copy in tg_copies:
        copy.wait_recv()
    for t in range(tiles):
        w_out_all[t * piece_rows:(t + 1) * piece_rows, :] = piece_all[t].astype(F32)
    done_copy.wait_recv()
    small_out[...] = small_done[...]

    for copy in face_copies + face_passes + rim_copies + rim_passes + rs_copies + dp_copies + sd_copies + tg_copies + st_copies + [
        win_copy, wout_copy, cg_copy, part_copy, small_copy, done_copy
    ]:
        copy.wait_send()


def in_hbm(array):
    return pltpu.with_memory_space_constraint(array, pltpu.MemorySpace.HBM)


def on_device(inputs, kernel, norm_gain, w_in, w_out, layer_scale, cotangent, adjacency):
    ts, ch = inputs.shape[2], inputs.shape[4]
    hid = w_in.shape[1]
    tiles, dps = lax.axis_size("tile"), lax.axis_size("dp")
    factor = 1.0 / math.sqrt(dps * tiles * ts * ts)
    strip = H * ts
    rim_rows = 2 * strip + 32
    piece = 2 * (ch // dps) // tiles
    half_small = SMALL_ROWS // 2
    part_rows = ch // dps
    vmem = pl.BlockSpec(memory_space=pltpu.VMEM)
    hbm = pl.BlockSpec(memory_space=pltpu.MemorySpace.HBM)
    dma = pltpu.SemaphoreType.DMA
    peers_t, peers_d = max(tiles - 1, 1), max(dps - 1, 1)
    out, small, grads = pl.pallas_call(
        functools.partial(body, tiles, dps, factor),
        out_shape=(
            jax.ShapeDtypeStruct((ts, ts, ch), BF16),
            jax.ShapeDtypeStruct((2, SMALL_ROWS // 2, ch), F32),
            jax.ShapeDtypeStruct((2 * part_rows, hid), F32),
        ),
        in_specs=[pl.BlockSpec(memory_space=pltpu.SMEM), hbm, hbm, vmem, vmem, hbm, hbm, vmem],
        out_specs=(vmem,) * 3,
        scratch_shapes=[
            pltpu.VMEM((ts + 2 * H, ts + 2 * COL, ch), F32),
            pltpu.VMEM((8, strip, ch), F32),
            pltpu.VMEM((tiles, 4, strip, ch), BF16),
            pltpu.VMEM((2, ch, hid), BF16),
            pltpu.VMEM((2, hid, ch), BF16),
            pltpu.VMEM((ts // 2, ts, ch), F32),
            pltpu.VMEM((2, 2, ch, hid), F32),
            pltpu.VMEM((ts, ts, ch), BF16),
            pltpu.VMEM((ts + 2 * (KS - 1) + 2, ts + 2 * COL, ch), F32),
            pltpu.VMEM((ts + 2 * H + 2, ts + 8, ch), F32),
            pltpu.VMEM((2, rim_rows, ch), F32),
            pltpu.VMEM((tiles, 2, rim_rows, ch), BF16),
            pltpu.VMEM((4, strip, ch), F32),
            pltpu.VMEM((2, ch, hid), F32),
            pltpu.VMEM((dps, 2, part_rows, hid), F32),
            pltpu.VMEM((dps, 2, part_rows, hid), F32),
            pltpu.VMEM((tiles, piece, hid), BF16),
            pltpu.VMEM((tiles, piece, hid), BF16),
            pltpu.VMEM((tiles, piece, hid), BF16),
            pltpu.VMEM((SMALL_ROWS, 8, ch), F32),
            pltpu.VMEM((2, half_small, ch), F32),
            pltpu.VMEM((half_small, ch), F32),
            pltpu.VMEM((dps, half_small, ch), F32),
            pltpu.VMEM((tiles, half_small, ch), F32),
            pltpu.VMEM((2, half_small, ch), F32),
            pltpu.VMEM((ts, ts, ch), F32),
            pltpu.VMEM((ts, ts, ch), BF16),
            pltpu.VMEM((ts, ts, ch), BF16),
            dma((4,)),
            dma((peers_t,)), dma((peers_t,)), dma((4 + 2 * tiles,)), dma((4 + 2 * tiles,)), dma((peers_t,)), dma((peers_t,)),
            dma((peers_d,)), dma((peers_d,)), dma((peers_t,)), dma((peers_t,)), dma((peers_t,)), dma((peers_t,)),
            dma((peers_d,)), dma((peers_d,)), dma((peers_t,)), dma((peers_t,)),
        ],
        compiler_params=pltpu.CompilerParams(
            collective_id=0, has_side_effects=True, vmem_limit_bytes=48 * 1024 * 1024
        ),
    )(
        jnp.transpose(adjacency, (0, 2, 1)), in_hbm(inputs[0, 0]), in_hbm(cotangent[0, 0]), kernel,
        norm_gain[None], in_hbm(w_in), in_hbm(w_out), layer_scale[None],
    )
    taps = KS * KS
    small = small.reshape(SMALL_ROWS, ch)
    return (
        out[None, None],
        small[:taps],
        small[taps],
        grads[:part_rows],
        grads[part_rows:].T,
        small[taps + 1],
    )


def solution(mesh):
    placed = (
        P(("group", "dp"), "tile", None, None, None),
        P(),
        P(),
        P(None, "chan"),
        P("chan", None),
        P(),
        P(("group", "dp"), "tile", None, None, None),
        P(),
    )
    return jax.shard_map(
        on_device,
        mesh=mesh,
        in_specs=placed,
        out_specs=(
            P(("group", "dp"), "tile", None, None, None),
            P("group", None),
            P("group"),
            P(("group", "dp"), "chan"),
            P(("group", "chan"), "dp"),
            P("group"),
        ),
        check_vma=False,
    )
```
